256 devices in a mesh: space: 64 (over y_hi, z, x), lag: 4 (over y_lo, core).
Axes of the slice: x: 4, y: 4 (y_hi: 2, y_lo: 2; y = y_hi * 2 + y_lo), z: 8, core: 2. Of those that a mesh axis runs over, the one named last changes fastest.
Arguments:
- prior: bfloat16 [8, 4, 64, 8192], P('lag', None, None, 'space'), may hold values from -6 to 6
- obs_value: float32 [65536], P('space'), may hold values from -6 to 6
- obs_weight: float32 [65536], P('space'), may hold values from 0.5 to 4
- obs_coef: float32 [4, 65536], P(None, 'space'), may hold values from 0.1 to 1
- obs_column: int32 [65536], P('space'), may hold values from 0 to 127
- obs_count: int32 [64], P('space'), may hold values from 512 to 1024
- halo_lists: int32 [2, 32768], P(None, 'space'), may hold values from 0 to 1023
- neighbours: int32 [64, 8192], P(None, 'space'), may hold values from 0 to 2047
- localization: float32 [64, 8192], P(None, 'space'), may hold values from 0.05 to 1
Outputs:
- analysis: bfloat16 [8, 4, 64, 8192], P('lag', None, None, 'space')
The draws below stay inside these ranges and needn't reach their ends.
Inputs may be any that keep to these rules, and one draw needn't show every extreme that they name: `obs_column`: each observation's column within its own tile. `obs_count`: slots at or beyond a tile's count hold no observation. `halo_lists`: slot numbers within the sending tile. `neighbours`: positions in the extended list of the column's tile.
All inputs are finite; a program needn't handle non-finite values.
Results may differ from the reference program's by a relative error of at most 0.0062.
Values may be sent and summed in bfloat16 or wider, within the bound.
No kernel may reach another device: no remote copies, remote signals or barrier semaphores. Data moves between devices by JAX's collectives and lax.ppermute only.
A program may use at most 64 MiB of HBM per device.

```python
import math
import jax
import jax.numpy as jnp
from jax import lax

K = 64
SPEC = 4
NB = 64
NSI = 2
COLS_DEV = 128
OBS_DEV = 1024
HALO = 512
TILES = 64
COLS = 8192
OBS = 65536
LAGS = 8


def place_ends(entries, own_key, smallest, high):
    spot = [jax.random.randint(jax.random.fold_in(own_key, axis), (), 0, length) for axis, length in enumerate(entries.shape)]
    widest = entries.shape.index(max(entries.shape))
    beside = spot[:widest] + [(spot[widest] + 1) % entries.shape[widest]] + spot[widest + 1:]
    return entries.at[tuple(spot)].set(smallest).at[tuple(beside)].set(high)


def block_scale(stream_key, extent, split, least, high):
    factor_of, own = 1.0, jax.random.fold_in(stream_key, 6)
    for axis_at, blocks in split:
        draws = jnp.exp(jax.random.uniform(jax.random.fold_in(own, axis_at), (blocks,), jnp.float32, least / len(split), high / len(split)))
        factor_of = factor_of * jnp.repeat(draws, extent[axis_at] // blocks).reshape([-1 if axis == axis_at else 1 for axis in range(len(extent))])
    return factor_of


def centred(rng, shape, scale, most, split=(), kind=jnp.bfloat16):
    level = block_scale(rng, shape, split, -0.22, 0.18) if split else 1.0
    drawn = jax.random.normal(rng, shape, jnp.float32) * scale * level
    return jnp.minimum(jnp.maximum(drawn, -most), most).astype(kind)


def setup_inputs(seed: int = 0) -> dict:
    streams_of = jax.random.split(jax.random.key(seed), 10)
    return {
        "prior": centred(streams_of[0], (LAGS, SPEC, K, COLS), 1.0, 6.0, ((0, 4), (3, 64))),
        "obs_value": centred(streams_of[1], (OBS,), 1.0, 6.0, ((0, 64),), jnp.float32),
        "obs_weight": jnp.clip(jnp.exp(math.log(4.0) - 2.0794415 * jax.random.uniform(streams_of[2], (OBS,), jnp.float32) ** block_scale(streams_of[2], (OBS,), ((0, 64),), -0.2, 0.2)), 0.5, 4.0),
        "obs_coef": jnp.clip(jnp.exp(math.log(1.0) - 2.3025851 * jax.random.uniform(streams_of[3], (SPEC, OBS), jnp.float32) ** block_scale(streams_of[3], (SPEC, OBS), ((1, 64),), -0.2, 0.2)), 0.1, 1.0),
        "obs_column": place_ends(jax.random.randint(streams_of[4], (OBS,), 0, COLS_DEV), jax.random.fold_in(streams_of[4], 1), 0, COLS_DEV - 1).astype(jnp.int32),
        "obs_count": place_ends(jax.random.randint(streams_of[5], (TILES,), HALO, OBS_DEV + 1), jax.random.fold_in(streams_of[5], 1), HALO, OBS_DEV).astype(jnp.int32),
        "halo_lists": place_ends(jax.random.randint(streams_of[6], (2, OBS // 2), 0, OBS_DEV), jax.random.fold_in(streams_of[6], 1), 0, OBS_DEV - 1).astype(jnp.int32),
        "neighbours": place_ends(jax.random.randint(streams_of[7], (NB, COLS), 0, OBS_DEV + 2 * HALO), jax.random.fold_in(streams_of[7], 1), 0, (OBS_DEV + 2 * HALO) - 1).astype(jnp.int32),
        "localization": jnp.clip(0.05 + 0.95 * jax.random.uniform(streams_of[8], (NB, COLS), jnp.float32) ** block_scale(streams_of[8], (NB, COLS), ((1, 64),), -0.2, 0.2), 0.05, 1.0),
    }


def matmul(left, right):
    return jnp.einsum('ikc,kjc->ijc', left, right, precision=lax.Precision.HIGHEST)

def observe(newest, coef, column, value, weight, count):
    picked = jnp.take(newest, column, axis=2).astype(jnp.float32)
    hx = lax.optimization_barrier(jnp.sum(coef[:, None, :] * picked, axis=0))
    mean_hx = lax.optimization_barrier(jnp.mean(hx, axis=0))
    valid = (jnp.arange(OBS_DEV) < count).astype(jnp.float32)
    pert = ((hx - mean_hx[None, :]) * valid[None, :]).astype(jnp.bfloat16)
    info = jnp.stack([weight * valid, (value - mean_hx) * valid]).astype(jnp.bfloat16)
    return (pert, info)

def solve(inputs):
    ext_pert, ext_info, table, local_weight = inputs
    gathered = jnp.take(ext_pert, table, axis=1)
    ginfo = jnp.take(ext_info, table, axis=1).astype(jnp.float32)
    weighted = (gathered.astype(jnp.float32) * (local_weight * ginfo[0])[None]).astype(jnp.bfloat16)
    gram = jnp.einsum('inc,jnc->ijc', gathered.astype(jnp.float32), weighted.astype(jnp.float32), precision=lax.Precision.HIGHEST)
    drive = jnp.einsum('inc,nc->ic', weighted.astype(jnp.float32), ginfo[1], precision=lax.Precision.HIGHEST)
    eye = jnp.eye(K, dtype=jnp.float32)[:, :, None]
    matrix = eye + gram / (K - 1)
    scale = jnp.sqrt(lax.optimization_barrier(jnp.sum(matrix * matrix, axis=(0, 1))))
    ycur = matrix / scale[None, None, :]
    zcur = jnp.broadcast_to(eye, matrix.shape)
    for step in range(NSI):
        smat = 1.5 * eye - 0.5 * matmul(zcur, ycur)
        ycur = matmul(ycur, smat)
        zcur = matmul(smat, zcur)
    inverse = matmul(zcur, zcur) / scale[None, None, :]
    mean_weight = jnp.einsum('ijc,jc->ic', inverse, drive, precision=lax.Precision.HIGHEST) / (K - 1)
    root = zcur / jnp.sqrt(scale)[None, None, :]
    return (root + mean_weight[:, None, :]).astype(jnp.bfloat16)

def reference(prior, obs_value, obs_weight, obs_coef, obs_column, obs_count, halo_lists, neighbours, localization):
    tiles = TILES
    newest = prior[LAGS - 1].reshape(SPEC, K, tiles, COLS_DEV).transpose(2, 0, 1, 3)
    coef = obs_coef.reshape(SPEC, tiles, OBS_DEV).transpose(1, 0, 2)
    pert, info = jax.vmap(observe)(newest, coef, obs_column.reshape(tiles, OBS_DEV), obs_value.reshape(tiles, OBS_DEV), obs_weight.reshape(tiles, OBS_DEV), obs_count)
    lists = halo_lists.reshape(2, tiles, HALO)
    pick = jax.vmap(lambda arr, idx: jnp.take(arr, idx, axis=1))
    up_pert, up_info = (pick(pert, lists[0]), pick(info, lists[0]))
    down_pert, down_info = (pick(pert, lists[1]), pick(info, lists[1]))
    zero_pert = jnp.zeros_like(up_pert[:1])
    zero_info = jnp.zeros_like(up_info[:1])
    below_pert = jnp.concatenate([zero_pert, up_pert[:-1]], axis=0)
    below_info = jnp.concatenate([zero_info, up_info[:-1]], axis=0)
    above_pert = jnp.concatenate([down_pert[1:], zero_pert], axis=0)
    above_info = jnp.concatenate([down_info[1:], zero_info], axis=0)
    ext_pert = jnp.concatenate([pert, below_pert, above_pert], axis=2)
    ext_info = jnp.concatenate([info, below_info, above_info], axis=2)
    table = neighbours.reshape(NB, tiles, COLS_DEV).transpose(1, 0, 2)
    local_weight = localization.reshape(NB, tiles, COLS_DEV).transpose(1, 0, 2)
    trans = lax.map(solve, (ext_pert, ext_info, table, local_weight))
    trans = trans.transpose(1, 2, 0, 3).reshape(K, K, COLS)
    values = prior.astype(jnp.float32)
    prior_mean = lax.optimization_barrier(jnp.mean(values, axis=2, keepdims=True))
    prior_pert = (values - prior_mean).astype(jnp.bfloat16)
    mixed = jnp.einsum('lskc,kjc->lsjc', prior_pert.astype(jnp.float32), trans.astype(jnp.float32), precision=lax.Precision.HIGHEST)
    return (prior_mean + mixed).astype(jnp.bfloat16)
```

```python
import functools

import jax
import jax.numpy as jnp
from jax import lax
from jax.experimental import pallas as pl
from jax.experimental.pallas import tpu as pltpu
from jax.sharding import PartitionSpec as P

K = 64
HALF = 64
ROWS = 80
INTERPRET = False
F32 = jnp.float32
BF16 = jnp.bfloat16


def lanes_of(shape):
    return lax.broadcasted_iota(jnp.int32, shape, len(shape) - 1)


def dot(left, right):
    return jnp.dot(left, right, preferred_element_type=F32)


def observe_kernel(flag, count, newest, coef, column, value, weight, lists, own, first, second):
    slots = column.shape[1]
    spec = newest.shape[0]
    halo = lists.shape[1]
    hot = lax.broadcasted_iota(jnp.int32, (128, slots), 0) == column[...]
    hot = jnp.where(hot, 1.0, 0.0).astype(BF16)
    picked = dot(newest[...].reshape(spec * K, 128), hot)
    hx = coef[0:1, :] * picked[0:K]
    for s in range(1, spec):
        hx = hx + coef[s : s + 1, :] * picked[s * K : (s + 1) * K]
    mean = jnp.sum(hx, axis=0, keepdims=True) * (1.0 / K)
    valid = jnp.where(lanes_of((1, slots)) < count[0], 1.0, 0.0)
    pert = (hx - mean) * valid
    info = jnp.concatenate(
        [weight[...] * valid, (value[...] - mean) * valid, jnp.zeros((ROWS - K - 2, slots), F32)],
        axis=0,
    )
    table = jnp.concatenate([pert, info], axis=0).astype(BF16)
    own[...] = table
    blocks = slots // 128
    stacked = jnp.concatenate([table[:, b * 128 : (b + 1) * 128] for b in range(blocks)], axis=0)
    odd = flag[0] == 1
    for out, mine, other in ((first, 0, 1), (second, 1, 0)):
        index = jnp.where(odd, lists[mine : mine + 1, :], lists[other : other + 1, :])
        low = index & 127
        high = index >> 7
        hot = lax.broadcasted_iota(jnp.int32, (128, halo), 0) == low
        found = dot(stacked, jnp.where(hot, 1.0, 0.0).astype(BF16))
        total = found[0:ROWS]
        for b in range(1, blocks):
            total = jnp.where(high == b, found[b * ROWS : (b + 1) * ROWS], total)
        out[...] = total.astype(BF16)


def packed(square, lower):
    left = lanes_of((HALF, 128)) < HALF
    if lower:
        return jnp.where(left, square[0:HALF], pltpu.roll(square[HALF:], HALF, 1))
    return jnp.where(left, pltpu.roll(square[0:HALF], HALF, 1), square[HALF:])


def block_diagonal(pair, left):
    zero = jnp.zeros_like(pair)
    return jnp.concatenate([jnp.where(left, pair, zero), jnp.where(left, zero, pair)], axis=0)


def solve_kernel(
    flag, index, own, first, second, local, prior, out,
    table_a, table_b, rows, matrix, squares, factors, pd, mixed, shift, means, weights,
):
    lags, spec = prior.shape[0], prior.shape[1]
    slots, halo = own.shape[1], first.shape[1]
    odd = flag[0]
    left = lanes_of((HALF, 128)) < HALF

    def put(source, offset, block):
        piece = source[:, block * 128 : (block + 1) * 128].astype(F32)
        piece = jnp.concatenate([piece, jnp.zeros((128 - ROWS, 128), F32)], axis=0).T
        at = pl.multiple_of(offset + block * 128, 128)
        table_a[pl.ds(at, 128), :] = piece
        table_b[pl.ds(at, 128), :] = pltpu.roll(piece, HALF, 1)

    for b in range(slots // 128):
        put(own, 0, b)
    for b in range(halo // 128):
        put(first, slots + odd * halo, b)
        put(second, slots + (1 - odd) * halo, b)

    twice = jnp.concatenate([local[...], local[...]], axis=0).T
    weights[...] = jnp.where(left, twice[0:HALF], twice[HALF:])

    def rank(pair):
        lag, s = pair // spec, pair % spec
        values = prior[lag, s].astype(F32)
        mean = jnp.sum(values, axis=0, keepdims=True) * (1.0 / K)
        means[pair : pair + 1, :] = mean
        return (values - mean).astype(BF16).astype(F32)

    count = lags * spec
    for pair in range(0, count, 2):
        square = jnp.concatenate([rank(pair), rank(pair + 1)], axis=0).T
        pd[pl.ds(pair, HALF, stride=16), :] = packed(square, True)
        pd[pl.ds(pair + 1, HALF, stride=16), :] = packed(square, False)

    row = lax.broadcasted_iota(jnp.int32, (HALF, 128), 0)
    eye = jnp.where(row == (lanes_of((HALF, 128)) & (HALF - 1)), 1.0, 0.0)
    leftb = lanes_of((HALF, 128)) < HALF
    ones = block_diagonal(jnp.ones((HALF, 128), F32), left).astype(BF16)

    @pl.loop(0, HALF)
    def _(q):
        for n in range(HALF):
            rows[n : n + 1, :] = table_a[pl.ds(index[n, q], 1), :]
            rows[HALF + n : HALF + n + 1, :] = table_b[pl.ds(index[n, q + HALF], 1), :]
        found = rows[...]
        across = found.T
        gathered = jnp.where(left, across[0:HALF], across[HALF:])
        top = left[0:1]
        info0 = jnp.where(top, across[HALF : HALF + 1], across[0:1])
        info1 = jnp.where(top, across[HALF + 1 : HALF + 2], across[1:2])
        scaled = weights[pl.ds(q, 1), :] * info0
        weighted = (gathered * scaled).astype(BF16)
        pull = scaled * info1
        pull_high = pull.astype(BF16).astype(F32)
        extra = jnp.concatenate([pull_high, pull - pull_high, jnp.zeros((14, 128), F32)], axis=0)
        lhs = jnp.concatenate([weighted, extra.astype(BF16)], axis=0)
        zero = jnp.zeros((HALF, 128), F32)
        diagonal = jnp.concatenate(
            [jnp.where(left, found[0:HALF], zero), jnp.where(left, zero, found[HALF:])], axis=0
        ).astype(BF16)
        product = dot(lhs, diagonal)
        full = eye + product[0:HALF] * (1.0 / (K - 1))
        matrix[q] = full
        squares[pl.ds(q, 1), :] = jnp.sum(full * full, axis=0, keepdims=True)
        drive = product[HALF : HALF + 1] + product[HALF + 1 : HALF + 2]
        drive_low = drive - drive.astype(BF16).astype(F32)
        tail = jnp.concatenate([drive, drive_low, jnp.zeros((6, 128), F32)], axis=0)
        pd[pl.ds(pl.multiple_of(q * 16 + 8, 8), 8), :] = tail

    def half_sums(values):
        high = values.astype(BF16)
        low = (values - high.astype(F32)).astype(BF16)
        return dot(high, ones) + dot(low, ones)

    scale = jnp.sqrt(half_sums(squares[...]))
    factors[...] = 1.0 / scale

    @pl.loop(0, HALF)
    def _(q):
        a = matrix[q] * factors[pl.ds(q, 1), :]
        ab = a.astype(BF16)
        b = dot(ab, block_diagonal(ab, leftb))
        c = -0.5625 * a + 0.0625 * b
        z = dot(c.astype(BF16), block_diagonal(b.astype(BF16), leftb))
        z = z + 2.25 * eye - 2.4375 * a + 1.6875 * b
        lhs = pd[pl.ds(pl.multiple_of(q * 16, 16), 16), :].astype(BF16)
        product = dot(lhs, block_diagonal(z.astype(BF16), leftb))
        mix = product[0:8]
        pulled = product[8:9] + product[9:10]
        at = pl.ds(pl.multiple_of(q * 8, 8), 8)
        mixed[at, :] = mix
        shift[at, :] = mix * pulled

    shift[...] = half_sums(shift[...])
    one = factors[...]
    root = jnp.sqrt(one)
    one = one * (1.0 / (K - 1))

    def final(pair):
        at = pl.ds(pair, HALF, stride=8)
        return mixed[at, :] * root + shift[at, :] * one

    for pair in range(0, count, 2):
        square = jnp.concatenate([final(pair), final(pair + 1)], axis=0).T
        for which in range(2):
            lag, s = (pair + which) // spec, (pair + which) % spec
            value = packed(square, which == 0) + means[pair + which : pair + which + 1, :]
            out[lag, s] = value.astype(BF16)


def vmem():
    return pl.BlockSpec(memory_space=pltpu.VMEM)


def smem():
    return pl.BlockSpec(memory_space=pltpu.SMEM)


def observe(flag, count, newest, coef, column, value, weight, lists):
    slots, halo = column.shape[0], lists.shape[1]
    shapes = [(ROWS, slots), (ROWS, halo), (ROWS, halo)]
    return pl.pallas_call(
        observe_kernel,
        out_shape=[jax.ShapeDtypeStruct(s, BF16) for s in shapes],
        in_specs=[smem(), smem()] + [vmem()] * 6,
        out_specs=[vmem()] * 3,
        interpret=INTERPRET,
        name="observe",
    )(flag, count, newest, coef, column[None], value[None], weight[None], lists)


def solve(flag, index, own, first, second, local, prior):
    positions = own.shape[1] + 2 * first.shape[1]
    return pl.pallas_call(
        solve_kernel,
        out_shape=jax.ShapeDtypeStruct(prior.shape, BF16),
        in_specs=[smem(), smem()] + [vmem()] * 5,
        out_specs=vmem(),
        scratch_shapes=[
            pltpu.VMEM((positions, 128), F32),
            pltpu.VMEM((positions, 128), F32),
            pltpu.VMEM((128, 128), F32),
            pltpu.VMEM((HALF, HALF, 128), F32),
            pltpu.VMEM((HALF, 128), F32),
            pltpu.VMEM((HALF, 128), F32),
            pltpu.VMEM((HALF * 16, 128), F32),
            pltpu.VMEM((HALF * 8, 128), F32),
            pltpu.VMEM((HALF * 8, 128), F32),
            pltpu.VMEM((8, 128), F32),
            pltpu.VMEM((HALF, 128), F32),
        ],
        interpret=INTERPRET,
        name="solve",
    )(flag, index, own, first, second, local, prior)


def swaps(length, start):
    pairs = []
    for low in range(start, length - 1, 2):
        pairs += [(low, low + 1), (low + 1, low)]
    return pairs


def body(
    prior,
    obs_value,
    obs_weight,
    obs_coef,
    obs_column,
    obs_count,
    halo_lists,
    neighbours,
    localization,
):
    lags = lax.axis_size("lag")
    tiles = lax.axis_size("space")
    flag = (lax.axis_index("space") % 2)[None].astype(jnp.int32)
    newest = lax.all_gather(prior[-1], "lag")[lags - 1]
    own, first, second = observe(
        flag, obs_count, newest, obs_coef, obs_column, obs_value, obs_weight, halo_lists
    )
    first = lax.ppermute(first, "space", swaps(tiles, 1))
    second = lax.ppermute(second, "space", swaps(tiles, 0))
    return solve(flag, neighbours, own, first, second, localization, prior)


def solution(mesh):
    return jax.shard_map(
        body,
        mesh=mesh,
        in_specs=(
            P("lag", None, None, "space"),
            P("space"),
            P("space"),
            P(None, "space"),
            P("space"),
            P("space"),
            P(None, "space"),
            P(None, "space"),
            P(None, "space"),
        ),
        out_specs=P("lag", None, None, "space"),
        check_vma=False,
    )
```

```python
import functools

import jax
import jax.numpy as jnp
from jax import lax
from jax.experimental import pallas as pl
from jax.experimental.pallas import tpu as pltpu
from jax.sharding import PartitionSpec as P

K = 64
HALF = 64
ROWS = 80
UA = 16
UC = 16
INTERPRET = False
F32 = jnp.float32
BF16 = jnp.bfloat16


def lanes_of(shape):
    return lax.broadcasted_iota(jnp.int32, shape, len(shape) - 1)


def dot(left, right):
    return jnp.dot(left, right, preferred_element_type=F32)


def observe_kernel(flag, count, newest, coef, column, value, weight, lists, own, first, second):
    slots = column.shape[1]
    spec = newest.shape[0]
    halo = lists.shape[1]
    hot = lax.broadcasted_iota(jnp.int32, (128, slots), 0) == column[...]
    hot = jnp.where(hot, 1.0, 0.0).astype(BF16)
    picked = dot(newest[...].reshape(spec * K, 128), hot)
    hx = coef[0:1, :] * picked[0:K]
    for s in range(1, spec):
        hx = hx + coef[s : s + 1, :] * picked[s * K : (s + 1) * K]
    mean = jnp.sum(hx, axis=0, keepdims=True) * (1.0 / K)
    valid = jnp.where(lanes_of((1, slots)) < count[0], 1.0, 0.0)
    pert = (hx - mean) * valid
    info = jnp.concatenate(
        [weight[...] * valid, (value[...] - mean) * valid, jnp.zeros((ROWS - K - 2, slots), F32)],
        axis=0,
    )
    table = jnp.concatenate([pert, info], axis=0).astype(BF16)
    own[...] = table
    blocks = slots // 128
    stacked = jnp.concatenate([table[:, b * 128 : (b + 1) * 128] for b in range(blocks)], axis=0)
    odd = flag[0] == 1
    for out, mine, other in ((first, 0, 1), (second, 1, 0)):
        index = jnp.where(odd, lists[mine : mine + 1, :], lists[other : other + 1, :])
        low = index & 127
        high = index >> 7
        hot = lax.broadcasted_iota(jnp.int32, (128, halo), 0) == low
        found = dot(stacked, jnp.where(hot, 1.0, 0.0).astype(BF16))
        total = found[0:ROWS]
        for b in range(1, blocks):
            total = jnp.where(high == b, found[b * ROWS : (b + 1) * ROWS], total)
        out[...] = total.astype(BF16)


def packed(square, lower):
    left = lanes_of((HALF, 128)) < HALF
    if lower:
        return jnp.where(left, square[0:HALF], pltpu.roll(square[HALF:], HALF, 1))
    return jnp.where(left, pltpu.roll(square[0:HALF], HALF, 1), square[HALF:])


def block_diagonal(pair, left):
    zero = jnp.zeros_like(pair)
    return jnp.concatenate([jnp.where(left, pair, zero), jnp.where(left, zero, pair)], axis=0)


def solve_kernel(
    flag, index, own, first, second, local, prior, out,
    table_a, table_b, rows, matrix, squares, factors, pd, mixed, shift, means, weights,
):
    lags, spec = prior.shape[0], prior.shape[1]
    slots, halo = own.shape[1], first.shape[1]
    odd = flag[0]
    left = lanes_of((HALF, 128)) < HALF

    def put(source, offset, block):
        piece = source[:, block * 128 : (block + 1) * 128].astype(F32)
        piece = jnp.concatenate([piece, jnp.zeros((128 - ROWS, 128), F32)], axis=0).T
        at = pl.multiple_of(offset + block * 128, 128)
        table_a[pl.ds(at, 128), :] = piece
        table_b[pl.ds(at, 128), :] = pltpu.roll(piece, HALF, 1)

    for b in range(slots // 128):
        put(own, 0, b)
    for b in range(halo // 128):
        put(first, slots + odd * halo, b)
        put(second, slots + (1 - odd) * halo, b)

    twice = jnp.concatenate([local[...], local[...]], axis=0).T
    weights[...] = jnp.where(left, twice[0:HALF], twice[HALF:])

    def rank(pair):
        lag, s = pair // spec, pair % spec
        values = prior[lag, s].astype(F32)
        mean = jnp.sum(values, axis=0, keepdims=True) * (1.0 / K)
        means[pair : pair + 1, :] = mean
        return (values - mean).astype(BF16).astype(F32)

    count = lags * spec
    for pair in range(0, count, 2):
        square = jnp.concatenate([rank(pair), rank(pair + 1)], axis=0).T
        pd[pl.ds(pair, HALF, stride=16), :] = packed(square, True)
        pd[pl.ds(pair + 1, HALF, stride=16), :] = packed(square, False)

    row = lax.broadcasted_iota(jnp.int32, (HALF, 128), 0)
    eye = jnp.where(row == (lanes_of((HALF, 128)) & (HALF - 1)), 1.0, 0.0)
    leftb = lanes_of((HALF, 128)) < HALF
    ones = block_diagonal(jnp.ones((HALF, 128), F32), left).astype(BF16)

    @pl.loop(0, HALF // UA)
    def _(step):
        qs = [step * UA + u for u in range(UA)]
        for u, q in enumerate(qs):
            for n in range(HALF):
                rows[u, n : n + 1, :] = table_a[pl.ds(index[n, q], 1), :]
                rows[u, HALF + n : HALF + n + 1, :] = table_b[pl.ds(index[n, q + HALF], 1), :]
        lefts, diagonals = [], []
        top = left[0:1]
        zero = jnp.zeros((HALF, 128), F32)
        for u, q in enumerate(qs):
            found = rows[u]
            across = found.T
            gathered = jnp.where(left, across[0:HALF], across[HALF:])
            info0 = jnp.where(top, across[HALF : HALF + 1], across[0:1])
            info1 = jnp.where(top, across[HALF + 1 : HALF + 2], across[1:2])
            scaled = weights[pl.ds(q, 1), :] * info0
            weighted = (gathered * scaled).astype(BF16)
            pull = scaled * info1
            pull_high = pull.astype(BF16).astype(F32)
            extra = jnp.concatenate([pull_high, pull - pull_high, jnp.zeros((14, 128), F32)], axis=0)
            lefts.append(jnp.concatenate([weighted, extra.astype(BF16)], axis=0))
            diagonals.append(jnp.concatenate(
                [jnp.where(left, found[0:HALF], zero), jnp.where(left, zero, found[HALF:])], axis=0
            ).astype(BF16))
        products = [dot(l, d) for l, d in zip(lefts, diagonals)]
        for q, product in zip(qs, products):
            full = eye + product[0:HALF] * (1.0 / (K - 1))
            matrix[q] = full
            squares[pl.ds(q, 1), :] = jnp.sum(full * full, axis=0, keepdims=True)
            drive = product[HALF : HALF + 1] + product[HALF + 1 : HALF + 2]
            drive_low = drive - drive.astype(BF16).astype(F32)
            tail = jnp.concatenate([drive, drive_low, jnp.zeros((6, 128), F32)], axis=0)
            pd[pl.ds(pl.multiple_of(q * 16 + 8, 8), 8), :] = tail

    def half_sums(values):
        high = values.astype(BF16)
        low = (values - high.astype(F32)).astype(BF16)
        return dot(high, ones) + dot(low, ones)

    scale = jnp.sqrt(half_sums(squares[...]))
    factors[...] = 1.0 / scale

    @pl.loop(0, HALF // UC)
    def _(step):
        qs = [step * UC + u for u in range(UC)]
        first_powers = [matrix[q] * factors[pl.ds(q, 1), :] for q in qs]
        halves = [a.astype(BF16) for a in first_powers]
        second_powers = [dot(a, block_diagonal(a, leftb)) for a in halves]
        mixes = [(-0.5625 * a + 0.0625 * b).astype(BF16) for a, b in zip(first_powers, second_powers)]
        zs = [dot(c, block_diagonal(b.astype(BF16), leftb)) for c, b in zip(mixes, second_powers)]
        zs = [
            z + 2.25 * eye - 2.4375 * a + 1.6875 * b
            for z, a, b in zip(zs, first_powers, second_powers)
        ]
        sides = [pd[pl.ds(pl.multiple_of(q * 16, 16), 16), :].astype(BF16) for q in qs]
        products = [dot(p, block_diagonal(z.astype(BF16), leftb)) for p, z in zip(sides, zs)]
        for q, product in zip(qs, products):
            mix = product[0:8]
            pulled = product[8:9] + product[9:10]
            at = pl.ds(pl.multiple_of(q * 8, 8), 8)
            mixed[at, :] = mix
            shift[at, :] = mix * pulled

    shift[...] = half_sums(shift[...])
    one = factors[...]
    root = jnp.sqrt(one)
    one = one * (1.0 / (K - 1))

    def final(pair):
        at = pl.ds(pair, HALF, stride=8)
        return mixed[at, :] * root + shift[at, :] * one

    for pair in range(0, count, 2):
        square = jnp.concatenate([final(pair), final(pair + 1)], axis=0).T
        for which in range(2):
            lag, s = (pair + which) // spec, (pair + which) % spec
            value = packed(square, which == 0) + means[pair + which : pair + which + 1, :]
            out[lag, s] = value.astype(BF16)


def vmem():
    return pl.BlockSpec(memory_space=pltpu.VMEM)


def smem():
    return pl.BlockSpec(memory_space=pltpu.SMEM)


def observe(flag, count, newest, coef, column, value, weight, lists):
    slots, halo = column.shape[0], lists.shape[1]
    shapes = [(ROWS, slots), (ROWS, halo), (ROWS, halo)]
    return pl.pallas_call(
        observe_kernel,
        out_shape=[jax.ShapeDtypeStruct(s, BF16) for s in shapes],
        in_specs=[smem(), smem()] + [vmem()] * 6,
        out_specs=[vmem()] * 3,
        interpret=INTERPRET,
        name="observe",
    )(flag, count, newest, coef, column[None], value[None], weight[None], lists)


def solve(flag, index, own, first, second, local, prior):
    positions = own.shape[1] + 2 * first.shape[1]
    return pl.pallas_call(
        solve_kernel,
        out_shape=jax.ShapeDtypeStruct(prior.shape, BF16),
        in_specs=[smem(), smem()] + [vmem()] * 5,
        out_specs=vmem(),
        scratch_shapes=[
            pltpu.VMEM((positions, 128), F32),
            pltpu.VMEM((positions, 128), F32),
            pltpu.VMEM((UA, 128, 128), F32),
            pltpu.VMEM((HALF, HALF, 128), F32),
            pltpu.VMEM((HALF, 128), F32),
            pltpu.VMEM((HALF, 128), F32),
            pltpu.VMEM((HALF * 16, 128), F32),
            pltpu.VMEM((HALF * 8, 128), F32),
            pltpu.VMEM((HALF * 8, 128), F32),
            pltpu.VMEM((8, 128), F32),
            pltpu.VMEM((HALF, 128), F32),
        ],
        interpret=INTERPRET,
        name="solve",
    )(flag, index, own, first, second, local, prior)


def swaps(length, start):
    pairs = []
    for low in range(start, length - 1, 2):
        pairs += [(low, low + 1), (low + 1, low)]
    return pairs


def body(
    prior,
    obs_value,
    obs_weight,
    obs_coef,
    obs_column,
    obs_count,
    halo_lists,
    neighbours,
    localization,
):
    lags = lax.axis_size("lag")
    tiles = lax.axis_size("space")
    flag = (lax.axis_index("space") % 2)[None].astype(jnp.int32)
    newest = lax.all_gather(prior[-1], "lag")[lags - 1]
    own, first, second = observe(
        flag, obs_count, newest, obs_coef, obs_column, obs_value, obs_weight, halo_lists
    )
    first = lax.ppermute(first, "space", swaps(tiles, 1))
    second = lax.ppermute(second, "space", swaps(tiles, 0))
    return solve(flag, neighbours, own, first, second, localization, prior)


def solution(mesh):
    return jax.shard_map(
        body,
        mesh=mesh,
        in_specs=(
            P("lag", None, None, "space"),
            P("space"),
            P("space"),
            P(None, "space"),
            P("space"),
            P("space"),
            P(None, "space"),
            P(None, "space"),
            P(None, "space"),
        ),
        out_specs=P("lag", None, None, "space"),
        check_vma=False,
    )
```

```python
import jax
import jax.numpy as jnp
from jax import lax
from jax.experimental import pallas as pl
from jax.experimental.pallas import tpu as pltpu
from jax.sharding import PartitionSpec as P


K = 64
HALF = 64
ROWS = 80
UA = 16
UC = 16
INTERPRET = False
OBSERVE_BYTES = 12 << 20
SOLVE_BYTES = 24 << 20
F32 = jnp.float32
BF16 = jnp.bfloat16


def lanes_of(shape):
    return lax.broadcasted_iota(jnp.int32, shape, len(shape) - 1)


def dot(left, right):
    return jnp.dot(left, right, preferred_element_type=F32)


def observe_kernel(flag, count, newest, coef, column, value, weight, lists, own, first, second):
    slots = column.shape[1]
    lags, spec = newest.shape[0], newest.shape[1]
    halo = lists.shape[1]
    hot = lax.broadcasted_iota(jnp.int32, (128, slots), 0) == column[...]
    hot = jnp.where(hot, 1.0, 0.0).astype(BF16)
    picked = dot(newest[lags - 1].reshape(spec * K, 128), hot)
    hx = coef[0:1, :] * picked[0:K]
    for s in range(1, spec):
        hx = hx + coef[s : s + 1, :] * picked[s * K : (s + 1) * K]
    mean = jnp.sum(hx, axis=0, keepdims=True) * (1.0 / K)
    valid = jnp.where(lanes_of((1, slots)) < count[0], 1.0, 0.0)
    pert = (hx - mean) * valid
    info = jnp.concatenate(
        [weight[...] * valid, (value[...] - mean) * valid, jnp.zeros((ROWS - K - 2, slots), F32)],
        axis=0,
    )
    table = jnp.concatenate([pert, info], axis=0).astype(BF16)
    own[...] = table
    blocks = slots // 128
    stacked = jnp.concatenate([table[:, b * 128 : (b + 1) * 128] for b in range(blocks)], axis=0)
    odd = flag[0] == 1
    for out, mine, other in ((first, 0, 1), (second, 1, 0)):
        index = jnp.where(odd, lists[mine : mine + 1, :], lists[other : other + 1, :])
        low = index & 127
        high = index >> 7
        hot = lax.broadcasted_iota(jnp.int32, (128, halo), 0) == low
        found = dot(stacked, jnp.where(hot, 1.0, 0.0).astype(BF16))
        total = found[0:ROWS]
        for b in range(1, blocks):
            total = jnp.where(high == b, found[b * ROWS : (b + 1) * ROWS], total)
        out[...] = total.astype(BF16)


def packed(square, lower):
    left = lanes_of((HALF, 128)) < HALF
    if lower:
        return jnp.where(left, square[0:HALF], pltpu.roll(square[HALF:], HALF, 1))
    return jnp.where(left, pltpu.roll(square[0:HALF], HALF, 1), square[HALF:])


def block_diagonal(pair, left):
    zero = jnp.zeros_like(pair)
    return jnp.concatenate([jnp.where(left, pair, zero), jnp.where(left, zero, pair)], axis=0)


def solve_kernel(
    flag, index, own, first, second, local, prior, out,
    table_a, table_b, rows, matrix, squares, factors, pd, mixed, shift, means, weights,
):
    lags, spec = prior.shape[0], prior.shape[1]
    slots, halo = own.shape[1], first.shape[1]
    odd = flag[0]
    left = lanes_of((HALF, 128)) < HALF

    def put(source, offset, block):
        piece = source[:, block * 128 : (block + 1) * 128].astype(F32)
        piece = jnp.concatenate([piece, jnp.zeros((128 - ROWS, 128), F32)], axis=0).T
        at = pl.multiple_of(offset + block * 128, 128)
        table_a[pl.ds(at, 128), :] = piece
        table_b[pl.ds(at, 128), :] = pltpu.roll(piece, HALF, 1)

    for b in range(slots // 128):
        put(own, 0, b)
    for b in range(halo // 128):
        put(first, slots + odd * halo, b)
        put(second, slots + (1 - odd) * halo, b)

    twice = jnp.concatenate([local[...], local[...]], axis=0).T
    weights[...] = jnp.where(left, twice[0:HALF], twice[HALF:])

    def rank(pair):
        lag, s = pair // spec, pair % spec
        values = prior[lag, s].astype(F32)
        mean = jnp.sum(values, axis=0, keepdims=True) * (1.0 / K)
        means[pair : pair + 1, :] = mean
        return (values - mean).astype(BF16).astype(F32)

    count = lags * spec
    for pair in range(0, count, 2):
        square = jnp.concatenate([rank(pair), rank(pair + 1)], axis=0).T
        pd[pl.ds(pair, HALF, stride=16), :] = packed(square, True)
        pd[pl.ds(pair + 1, HALF, stride=16), :] = packed(square, False)

    row = lax.broadcasted_iota(jnp.int32, (HALF, 128), 0)
    eye = jnp.where(row == (lanes_of((HALF, 128)) & (HALF - 1)), 1.0, 0.0)
    leftb = lanes_of((HALF, 128)) < HALF
    ones = block_diagonal(jnp.ones((HALF, 128), F32), left).astype(BF16)

    @pl.loop(0, HALF // UA)
    def _(step):
        qs = [step * UA + u for u in range(UA)]
        for u, q in enumerate(qs):
            for n in range(HALF):
                rows[u, n : n + 1, :] = table_a[pl.ds(index[n, q], 1), :]
                rows[u, HALF + n : HALF + n + 1, :] = table_b[pl.ds(index[n, q + HALF], 1), :]
        lefts, diagonals = [], []
        top = left[0:1]
        zero = jnp.zeros((HALF, 128), F32)
        for u, q in enumerate(qs):
            found = rows[u]
            across = found.T
            gathered = jnp.where(left, across[0:HALF], across[HALF:])
            info0 = jnp.where(top, across[HALF : HALF + 1], across[0:1])
            info1 = jnp.where(top, across[HALF + 1 : HALF + 2], across[1:2])
            scaled = weights[pl.ds(q, 1), :] * info0
            weighted = (gathered * scaled).astype(BF16)
            pull = scaled * info1
            pull_high = pull.astype(BF16).astype(F32)
            extra = jnp.concatenate([pull_high, pull - pull_high, jnp.zeros((14, 128), F32)], axis=0)
            lefts.append(jnp.concatenate([weighted, extra.astype(BF16)], axis=0))
            diagonals.append(jnp.concatenate(
                [jnp.where(left, found[0:HALF], zero), jnp.where(left, zero, found[HALF:])], axis=0
            ).astype(BF16))
        products = [dot(l, d) for l, d in zip(lefts, diagonals)]
        for q, product in zip(qs, products):
            full = eye + product[0:HALF] * (1.0 / (K - 1))
            matrix[q] = full
            squares[pl.ds(q, 1), :] = jnp.sum(full * full, axis=0, keepdims=True)
            drive = product[HALF : HALF + 1] + product[HALF + 1 : HALF + 2]
            drive_low = drive - drive.astype(BF16).astype(F32)
            tail = jnp.concatenate([drive, drive_low, jnp.zeros((6, 128), F32)], axis=0)
            pd[pl.ds(pl.multiple_of(q * 16 + 8, 8), 8), :] = tail

    def half_sums(values):
        high = values.astype(BF16)
        low = (values - high.astype(F32)).astype(BF16)
        return dot(high, ones) + dot(low, ones)

    scale = jnp.sqrt(half_sums(squares[...]))
    factors[...] = 1.0 / scale

    @pl.loop(0, HALF // UC)
    def _(step):
        qs = [step * UC + u for u in range(UC)]
        first_powers = [matrix[q] * factors[pl.ds(q, 1), :] for q in qs]
        halves = [a.astype(BF16) for a in first_powers]
        second_powers = [dot(a, block_diagonal(a, leftb)) for a in halves]
        mixes = [(-0.5625 * a + 0.0625 * b).astype(BF16) for a, b in zip(first_powers, second_powers)]
        zs = [dot(c, block_diagonal(b.astype(BF16), leftb)) for c, b in zip(mixes, second_powers)]
        zs = [
            z + 2.25 * eye - 2.4375 * a + 1.6875 * b
            for z, a, b in zip(zs, first_powers, second_powers)
        ]
        sides = [pd[pl.ds(pl.multiple_of(q * 16, 16), 16), :].astype(BF16) for q in qs]
        products = [dot(p, block_diagonal(z.astype(BF16), leftb)) for p, z in zip(sides, zs)]
        for q, product in zip(qs, products):
            mix = product[0:8]
            pulled = product[8:9] + product[9:10]
            at = pl.ds(pl.multiple_of(q * 8, 8), 8)
            mixed[at, :] = mix
            shift[at, :] = mix * pulled

    shift[...] = half_sums(shift[...])
    one = factors[...]
    root = jnp.sqrt(one)
    one = one * (1.0 / (K - 1))

    def final(pair):
        at = pl.ds(pair, HALF, stride=8)
        return mixed[at, :] * root + shift[at, :] * one

    for pair in range(0, count, 2):
        square = jnp.concatenate([final(pair), final(pair + 1)], axis=0).T
        for which in range(2):
            lag, s = (pair + which) // spec, (pair + which) % spec
            value = packed(square, which == 0) + means[pair + which : pair + which + 1, :]
            out[lag, s] = value.astype(BF16)


def vmem():
    return pl.BlockSpec(memory_space=pltpu.VMEM)


def smem():
    return pl.BlockSpec(memory_space=pltpu.SMEM)


def observe(flag, count, newest, coef, column, value, weight, lists):
    slots, halo = column.shape[0], lists.shape[1]
    shapes = [(ROWS, slots), (ROWS, halo), (ROWS, halo)]
    return pl.pallas_call(
        observe_kernel,
        out_shape=[jax.ShapeDtypeStruct(s, BF16) for s in shapes],
        in_specs=[smem(), smem()] + [vmem()] * 6,
        out_specs=[vmem()] * 3,
        compiler_params=pltpu.CompilerParams(vmem_limit_bytes=OBSERVE_BYTES),
        interpret=INTERPRET,
        name="observe",
    )(flag, count, newest, coef, column[None], value[None], weight[None], lists)


def solve(flag, index, own, first, second, local, prior):
    positions = own.shape[1] + 2 * first.shape[1]
    return pl.pallas_call(
        solve_kernel,
        out_shape=jax.ShapeDtypeStruct(prior.shape, BF16),
        in_specs=[smem(), smem()] + [vmem()] * 5,
        out_specs=vmem(),
        scratch_shapes=[
            pltpu.VMEM((positions, 128), F32),
            pltpu.VMEM((positions, 128), F32),
            pltpu.VMEM((UA, 128, 128), F32),
            pltpu.VMEM((HALF, HALF, 128), F32),
            pltpu.VMEM((HALF, 128), F32),
            pltpu.VMEM((HALF, 128), F32),
            pltpu.VMEM((HALF * 16, 128), F32),
            pltpu.VMEM((HALF * 8, 128), F32),
            pltpu.VMEM((HALF * 8, 128), F32),
            pltpu.VMEM((8, 128), F32),
            pltpu.VMEM((HALF, 128), F32),
        ],
        compiler_params=pltpu.CompilerParams(vmem_limit_bytes=SOLVE_BYTES),
        interpret=INTERPRET,
        name="solve",
    )(flag, index, own, first, second, local, prior)


def swaps(length, start):
    pairs = []
    for low in range(start, length - 1, 2):
        pairs += [(low, low + 1), (low + 1, low)]
    return pairs


def body(
    prior,
    obs_value,
    obs_weight,
    obs_coef,
    obs_column,
    obs_count,
    halo_lists,
    neighbours,
    localization,
):
    tiles = lax.axis_size("space")
    flag = (lax.axis_index("space") % 2)[None].astype(jnp.int32)
    newest = lax.all_gather(prior[-1], "lag")
    own, first, second = observe(
        flag, obs_count, newest, obs_coef, obs_column, obs_value, obs_weight, halo_lists
    )
    second = lax.ppermute(second, "space", swaps(tiles, 0))
    first = lax.ppermute(first, "space", swaps(tiles, 1))
    return solve(flag, neighbours, own, first, second, localization, prior)


def solution(mesh):
    return jax.shard_map(
        body,
        mesh=mesh,
        in_specs=(
            P("lag", None, None, "space"),
            P("space"),
            P("space"),
            P(None, "space"),
            P("space"),
            P("space"),
            P(None, "space"),
            P(None, "space"),
            P(None, "space"),
        ),
        out_specs=P("lag", None, None, "space"),
        check_vma=False,
    )
```

```python
import jax
import jax.numpy as jnp
from jax import lax
from jax.experimental import pallas as pl
from jax.experimental.pallas import tpu as pltpu
from jax.sharding import PartitionSpec as P


K = 64
HALF = 64
ROWS = 80
UA = 32
UC = 32
INTERPRET = False
OBSERVE_BYTES = 12 << 20
SOLVE_BYTES = 24 << 20
F32 = jnp.float32
BF16 = jnp.bfloat16


def lanes_of(shape):
    return lax.broadcasted_iota(jnp.int32, shape, len(shape) - 1)


def dot(left, right):
    return jnp.dot(left, right, preferred_element_type=F32)


def observe_kernel(flag, count, newest, coef, column, value, weight, lists, own, first, second):
    slots = column.shape[1]
    lags, spec = newest.shape[0], newest.shape[1]
    halo = lists.shape[1]
    hot = lax.broadcasted_iota(jnp.int32, (128, slots), 0) == column[...]
    hot = jnp.where(hot, 1.0, 0.0).astype(BF16)
    picked = dot(newest[lags - 1].reshape(spec * K, 128), hot)
    hx = coef[0:1, :] * picked[0:K]
    for s in range(1, spec):
        hx = hx + coef[s : s + 1, :] * picked[s * K : (s + 1) * K]
    mean = jnp.sum(hx, axis=0, keepdims=True) * (1.0 / K)
    valid = jnp.where(lanes_of((1, slots)) < count[0], 1.0, 0.0)
    pert = (hx - mean) * valid
    info = jnp.concatenate(
        [weight[...] * valid, (value[...] - mean) * valid, jnp.zeros((ROWS - K - 2, slots), F32)],
        axis=0,
    )
    table = jnp.concatenate([pert, info], axis=0).astype(BF16)
    own[...] = table
    blocks = slots // 128
    stacked = jnp.concatenate([table[:, b * 128 : (b + 1) * 128] for b in range(blocks)], axis=0)
    odd = flag[0] == 1
    for out, mine, other in ((first, 0, 1), (second, 1, 0)):
        index = jnp.where(odd, lists[mine : mine + 1, :], lists[other : other + 1, :])
        low = index & 127
        high = index >> 7
        hot = lax.broadcasted_iota(jnp.int32, (128, halo), 0) == low
        found = dot(stacked, jnp.where(hot, 1.0, 0.0).astype(BF16))
        total = found[0:ROWS]
        for b in range(1, blocks):
            total = jnp.where(high == b, found[b * ROWS : (b + 1) * ROWS], total)
        out[...] = total.astype(BF16)


def packed(square, lower):
    left = lanes_of((HALF, 128)) < HALF
    if lower:
        return jnp.where(left, square[0:HALF], pltpu.roll(square[HALF:], HALF, 1))
    return jnp.where(left, pltpu.roll(square[0:HALF], HALF, 1), square[HALF:])


def block_diagonal(pair, left):
    zero = jnp.zeros_like(pair)
    return jnp.concatenate([jnp.where(left, pair, zero), jnp.where(left, zero, pair)], axis=0)


def solve_kernel(
    flag, index, own, first, second, local, prior, out,
    matrix, squares, factors, pd, mixed, shift, means, weights, lows, codes,
):
    lags, spec = prior.shape[0], prior.shape[1]
    halo = first.shape[1]
    odd = flag[0]
    left = lanes_of((HALF, 128)) < HALF

    def beside(values):
        twice = jnp.concatenate([values, values], axis=0).T
        return jnp.where(left, twice[0:HALF], twice[HALF:])

    weights[...] = beside(local[...])
    places = beside(index[...].astype(F32)).astype(jnp.int32)
    block = places >> 9
    lows[...] = (places & 511).astype(F32)
    codes[...] = jnp.where(block >= 2, block ^ odd, block)

    def rank(pair):
        lag, s = pair // spec, pair % spec
        values = prior[lag, s].astype(F32)
        mean = jnp.sum(values, axis=0, keepdims=True) * (1.0 / K)
        means[pair : pair + 1, :] = mean
        return (values - mean).astype(BF16).astype(F32)

    count = lags * spec
    for pair in range(0, count, 2):
        square = jnp.concatenate([rank(pair), rank(pair + 1)], axis=0).T
        pd[pl.ds(pair, HALF, stride=16), :] = packed(square, True)
        pd[pl.ds(pair + 1, HALF, stride=16), :] = packed(square, False)

    row = lax.broadcasted_iota(jnp.int32, (HALF, 128), 0)
    eye = jnp.where(row == (lanes_of((HALF, 128)) & (HALF - 1)), 1.0, 0.0)
    leftb = lanes_of((HALF, 128)) < HALF
    ones = block_diagonal(jnp.ones((HALF, 128), F32), left).astype(BF16)

    stacked = jnp.concatenate(
        [own[:, 0:halo], own[:, halo:], first[...], second[...]], axis=0
    )
    counts = lax.broadcasted_iota(jnp.int32, (256, 256), 0).astype(F32).astype(BF16)

    def pick(q):
        low = jnp.concatenate([lows[pl.ds(q, 1), :], lows[pl.ds(q + 1, 1), :]], axis=1)
        code = jnp.concatenate([codes[pl.ds(q, 1), :], codes[pl.ds(q + 1, 1), :]], axis=1)
        hot = [
            jnp.where(counts == (low - 256.0 * h).astype(BF16), 1.0, 0.0).astype(BF16)
            for h in range(halo // 256)
        ]
        found = dot(stacked, jnp.concatenate(hot, axis=0))
        total = found[0:ROWS]
        for b in range(1, 4):
            total = jnp.where(code == b, found[b * ROWS : (b + 1) * ROWS], total)
        return total[:, 0:128], total[:, 128:]

    @pl.loop(0, HALF // UA)
    def _(step):
        qs = [step * UA + u for u in range(UA)]
        picked = []
        for q in qs[::2]:
            picked += pick(q)
        lefts, diagonals = [], []
        for q, found in zip(qs, picked):
            gathered = found[0:HALF]
            scaled = weights[pl.ds(q, 1), :] * found[HALF : HALF + 1]
            weighted = (gathered * scaled).astype(BF16)
            pull = scaled * found[HALF + 1 : HALF + 2]
            pull_high = pull.astype(BF16).astype(F32)
            extra = jnp.concatenate([pull_high, pull - pull_high, jnp.zeros((14, 128), F32)], axis=0)
            lefts.append(jnp.concatenate([weighted, extra.astype(BF16)], axis=0))
            diagonals.append(block_diagonal(gathered.astype(BF16), leftb))
        products = [
            lax.dot_general(l, d, (((1,), (1,)), ((), ())), preferred_element_type=F32)
            for l, d in zip(lefts, diagonals)
        ]
        for q, product in zip(qs, products):
            full = eye + product[0:HALF] * (1.0 / (K - 1))
            matrix[q] = full
            squares[pl.ds(q, 1), :] = jnp.sum(full * full, axis=0, keepdims=True)
            drive = product[HALF : HALF + 1] + product[HALF + 1 : HALF + 2]
            drive_low = drive - drive.astype(BF16).astype(F32)
            tail = jnp.concatenate([drive, drive_low, jnp.zeros((6, 128), F32)], axis=0)
            pd[pl.ds(pl.multiple_of(q * 16 + 8, 8), 8), :] = tail

    def half_sums(values):
        high = values.astype(BF16)
        low = (values - high.astype(F32)).astype(BF16)
        return dot(high, ones) + dot(low, ones)

    scale = jnp.sqrt(half_sums(squares[...]))
    factors[...] = 1.0 / scale

    @pl.loop(0, HALF // UC)
    def _(step):
        qs = [step * UC + u for u in range(UC)]
        first_powers = [matrix[q] * factors[pl.ds(q, 1), :] for q in qs]
        halves = [a.astype(BF16) for a in first_powers]
        second_powers = [dot(a, block_diagonal(a, leftb)) for a in halves]
        mixes = [(-0.5625 * a + 0.0625 * b).astype(BF16) for a, b in zip(first_powers, second_powers)]
        zs = [dot(c, block_diagonal(b.astype(BF16), leftb)) for c, b in zip(mixes, second_powers)]
        zs = [
            z + 2.25 * eye - 2.4375 * a + 1.6875 * b
            for z, a, b in zip(zs, first_powers, second_powers)
        ]
        sides = [pd[pl.ds(pl.multiple_of(q * 16, 16), 16), :].astype(BF16) for q in qs]
        products = [dot(p, block_diagonal(z.astype(BF16), leftb)) for p, z in zip(sides, zs)]
        for q, product in zip(qs, products):
            mix = product[0:8]
            pulled = product[8:9] + product[9:10]
            at = pl.ds(pl.multiple_of(q * 8, 8), 8)
            mixed[at, :] = mix
            shift[at, :] = mix * pulled

    shift[...] = half_sums(shift[...])
    one = factors[...]
    root = jnp.sqrt(one)
    one = one * (1.0 / (K - 1))

    def final(pair):
        at = pl.ds(pair, HALF, stride=8)
        return mixed[at, :] * root + shift[at, :] * one

    for pair in range(0, count, 2):
        square = jnp.concatenate([final(pair), final(pair + 1)], axis=0).T
        for which in range(2):
            lag, s = (pair + which) // spec, (pair + which) % spec
            value = packed(square, which == 0) + means[pair + which : pair + which + 1, :]
            out[lag, s] = value.astype(BF16)


def vmem():
    return pl.BlockSpec(memory_space=pltpu.VMEM)


def smem():
    return pl.BlockSpec(memory_space=pltpu.SMEM)


def observe(flag, count, newest, coef, column, value, weight, lists):
    slots, halo = column.shape[0], lists.shape[1]
    shapes = [(ROWS, slots), (ROWS, halo), (ROWS, halo)]
    return pl.pallas_call(
        observe_kernel,
        out_shape=[jax.ShapeDtypeStruct(s, BF16) for s in shapes],
        in_specs=[smem(), smem()] + [vmem()] * 6,
        out_specs=[vmem()] * 3,
        compiler_params=pltpu.CompilerParams(vmem_limit_bytes=OBSERVE_BYTES),
        interpret=INTERPRET,
        name="observe",
    )(flag, count, newest, coef, column[None], value[None], weight[None], lists)


def solve(flag, index, own, first, second, local, prior):
    return pl.pallas_call(
        solve_kernel,
        out_shape=jax.ShapeDtypeStruct(prior.shape, BF16),
        in_specs=[smem()] + [vmem()] * 6,
        out_specs=vmem(),
        scratch_shapes=[
            pltpu.VMEM((HALF, HALF, 128), F32),
            pltpu.VMEM((HALF, 128), F32),
            pltpu.VMEM((HALF, 128), F32),
            pltpu.VMEM((HALF * 16, 128), F32),
            pltpu.VMEM((HALF * 8, 128), F32),
            pltpu.VMEM((HALF * 8, 128), F32),
            pltpu.VMEM((8, 128), F32),
            pltpu.VMEM((HALF, 128), F32),
            pltpu.VMEM((HALF, 128), F32),
            pltpu.VMEM((HALF, 128), jnp.int32),
        ],
        compiler_params=pltpu.CompilerParams(vmem_limit_bytes=SOLVE_BYTES),
        interpret=INTERPRET,
        name="solve",
    )(flag, index, own, first, second, local, prior)


def swaps(length, start):
    pairs = []
    for low in range(start, length - 1, 2):
        pairs += [(low, low + 1), (low + 1, low)]
    return pairs


def body(
    prior,
    obs_value,
    obs_weight,
    obs_coef,
    obs_column,
    obs_count,
    halo_lists,
    neighbours,
    localization,
):
    tiles = lax.axis_size("space")
    flag = (lax.axis_index("space") % 2)[None].astype(jnp.int32)
    newest = lax.all_gather(prior[-1], "lag")
    own, first, second = observe(
        flag, obs_count, newest, obs_coef, obs_column, obs_value, obs_weight, halo_lists
    )
    second = lax.ppermute(second, "space", swaps(tiles, 0))
    first = lax.ppermute(first, "space", swaps(tiles, 1))
    return solve(flag, neighbours, own, first, second, localization, prior)


def solution(mesh):
    return jax.shard_map(
        body,
        mesh=mesh,
        in_specs=(
            P("lag", None, None, "space"),
            P("space"),
            P("space"),
            P(None, "space"),
            P("space"),
            P("space"),
            P(None, "space"),
            P(None, "space"),
            P(None, "space"),
        ),
        out_specs=P("lag", None, None, "space"),
        check_vma=False,
    )
```

```python
import jax
import jax.numpy as jnp
from jax import lax
from jax.experimental import pallas as pl
from jax.experimental.pallas import tpu as pltpu
from jax.sharding import PartitionSpec as P


K = 64
HALF = 64
ROWS = 80
UA = 32
UC = 32
INTERPRET = False
OBSERVE_BYTES = 12 << 20
SOLVE_BYTES = 24 << 20
F32 = jnp.float32
BF16 = jnp.bfloat16


def lanes_of(shape):
    return lax.broadcasted_iota(jnp.int32, shape, len(shape) - 1)


def dot(left, right):
    return jnp.dot(left, right, preferred_element_type=F32)


def stage_kernel(
    prior, coef, column, value, weight, lists, count,
    newest_out, coef_out, column_out, value_out, weight_out, lists_out, count_out,
    scalar, sems,
):
    lags = prior.shape[0]
    moves = (
        (prior.at[pl.ds(lags - 1, 1)], newest_out),
        (coef, coef_out),
        (column, column_out),
        (value, value_out),
        (weight, weight_out),
        (lists, lists_out),
        (count, scalar),
    )
    copies = [pltpu.make_async_copy(a, b, sems.at[n]) for n, (a, b) in enumerate(moves)]
    for copy in copies:
        copy.start()
    for copy in copies:
        copy.wait()
    count_out[...] = jnp.full((1, 128), scalar[0], jnp.int32)


def observe_kernel(flag, newest, coef, column, value, weight, lists, count, own, first, second):
    slots = column.shape[1]
    lags, spec = newest.shape[0], newest.shape[1]
    halo = lists.shape[1]
    hot = lax.broadcasted_iota(jnp.int32, (128, slots), 0) == column[...]
    hot = jnp.where(hot, 1.0, 0.0).astype(BF16)
    picked = dot(newest[lags - 1].reshape(spec * K, 128), hot)
    hx = coef[0:1, :] * picked[0:K]
    for s in range(1, spec):
        hx = hx + coef[s : s + 1, :] * picked[s * K : (s + 1) * K]
    mean = jnp.sum(hx, axis=0, keepdims=True) * (1.0 / K)
    valid = jnp.where(lanes_of((1, slots)) < count[:, 0:1], 1.0, 0.0)
    pert = (hx - mean) * valid
    info = jnp.concatenate(
        [weight[...] * valid, (value[...] - mean) * valid, jnp.zeros((ROWS - K - 2, slots), F32)],
        axis=0,
    )
    table = jnp.concatenate([pert, info], axis=0).astype(BF16)
    own[...] = table
    blocks = slots // 128
    stacked = jnp.concatenate([table[:, b * 128 : (b + 1) * 128] for b in range(blocks)], axis=0)
    odd = flag[0] == 1
    for out, mine, other in ((first, 0, 1), (second, 1, 0)):
        index = jnp.where(odd, lists[mine : mine + 1, :], lists[other : other + 1, :])
        low = index & 127
        high = index >> 7
        hot = lax.broadcasted_iota(jnp.int32, (128, halo), 0) == low
        found = dot(stacked, jnp.where(hot, 1.0, 0.0).astype(BF16))
        total = found[0:ROWS]
        for b in range(1, blocks):
            total = jnp.where(high == b, found[b * ROWS : (b + 1) * ROWS], total)
        out[...] = total.astype(BF16)


def packed(square, lower):
    left = lanes_of((HALF, 128)) < HALF
    if lower:
        return jnp.where(left, square[0:HALF], pltpu.roll(square[HALF:], HALF, 1))
    return jnp.where(left, pltpu.roll(square[0:HALF], HALF, 1), square[HALF:])


def block_diagonal(pair, left):
    zero = jnp.zeros_like(pair)
    return jnp.concatenate([jnp.where(left, pair, zero), jnp.where(left, zero, pair)], axis=0)


def prepare_kernel(flag, index, local, prior, pd, means, weights, lows, codes):
    lags, spec = prior.shape[0], prior.shape[1]
    left = lanes_of((HALF, 128)) < HALF

    def beside(values):
        twice = jnp.concatenate([values, values], axis=0).T
        return jnp.where(left, twice[0:HALF], twice[HALF:])

    weights[...] = beside(local[...])
    places = beside(index[...].astype(F32)).astype(jnp.int32)
    block = places >> 9
    lows[...] = (places & 511).astype(F32)
    codes[...] = jnp.where(block >= 2, block ^ flag[0], block)

    def rank(pair):
        lag, s = pair // spec, pair % spec
        values = prior[lag, s].astype(F32)
        mean = jnp.sum(values, axis=0, keepdims=True) * (1.0 / K)
        means[pair : pair + 1, :] = mean
        return (values - mean).astype(BF16).astype(F32)

    for pair in range(0, lags * spec, 2):
        square = jnp.concatenate([rank(pair), rank(pair + 1)], axis=0).T
        pd[pl.ds(pair, HALF, stride=8), :] = packed(square, True)
        pd[pl.ds(pair + 1, HALF, stride=8), :] = packed(square, False)


def solve_kernel(
    own, first, second, pd, means, weights, lows, codes, out,
    matrix, squares, factors, tails, mixed, shift,
):
    lags, spec = out.shape[0], out.shape[1]
    count = lags * spec
    halo = first.shape[1]
    left = lanes_of((HALF, 128)) < HALF

    row = lax.broadcasted_iota(jnp.int32, (HALF, 128), 0)
    eye = jnp.where(row == (lanes_of((HALF, 128)) & (HALF - 1)), 1.0, 0.0)
    leftb = lanes_of((HALF, 128)) < HALF
    ones = block_diagonal(jnp.ones((HALF, 128), F32), left).astype(BF16)

    stacked = jnp.concatenate(
        [own[:, 0:halo], own[:, halo:], first[...], second[...]], axis=0
    )
    counts = lax.broadcasted_iota(jnp.int32, (256, 256), 0).astype(F32).astype(BF16)

    def pick(q):
        low = jnp.concatenate([lows[pl.ds(q, 1), :], lows[pl.ds(q + 1, 1), :]], axis=1)
        code = jnp.concatenate([codes[pl.ds(q, 1), :], codes[pl.ds(q + 1, 1), :]], axis=1)
        hot = [
            jnp.where(counts == (low - 256.0 * h).astype(BF16), 1.0, 0.0).astype(BF16)
            for h in range(halo // 256)
        ]
        found = dot(stacked, jnp.concatenate(hot, axis=0))
        total = found[0:ROWS]
        for b in range(1, 4):
            total = jnp.where(code == b, found[b * ROWS : (b + 1) * ROWS], total)
        return total[:, 0:128], total[:, 128:]

    @pl.loop(0, HALF // UA)
    def _(step):
        qs = [step * UA + u for u in range(UA)]
        picked = []
        for q in qs[::2]:
            picked += pick(q)
        lefts, diagonals = [], []
        for q, found in zip(qs, picked):
            gathered = found[0:HALF]
            scaled = weights[pl.ds(q, 1), :] * found[HALF : HALF + 1]
            weighted = (gathered * scaled).astype(BF16)
            pull = scaled * found[HALF + 1 : HALF + 2]
            pull_high = pull.astype(BF16).astype(F32)
            extra = jnp.concatenate([pull_high, pull - pull_high, jnp.zeros((14, 128), F32)], axis=0)
            lefts.append(jnp.concatenate([weighted, extra.astype(BF16)], axis=0))
            diagonals.append(block_diagonal(gathered.astype(BF16), leftb))
        products = [
            lax.dot_general(l, d, (((1,), (1,)), ((), ())), preferred_element_type=F32)
            for l, d in zip(lefts, diagonals)
        ]
        for q, product in zip(qs, products):
            full = eye + product[0:HALF] * (1.0 / (K - 1))
            matrix[q] = full
            squares[pl.ds(q, 1), :] = jnp.sum(full * full, axis=0, keepdims=True)
            drive = product[HALF : HALF + 1] + product[HALF + 1 : HALF + 2]
            drive_low = drive - drive.astype(BF16).astype(F32)
            tail = jnp.concatenate([drive, drive_low, jnp.zeros((6, 128), F32)], axis=0)
            tails[pl.ds(pl.multiple_of(q * 8, 8), 8), :] = tail

    def half_sums(values):
        high = values.astype(BF16)
        low = (values - high.astype(F32)).astype(BF16)
        return dot(high, ones) + dot(low, ones)

    scale = jnp.sqrt(half_sums(squares[...]))
    factors[...] = 1.0 / scale

    @pl.loop(0, HALF // UC)
    def _(step):
        qs = [step * UC + u for u in range(UC)]
        first_powers = [matrix[q] * factors[pl.ds(q, 1), :] for q in qs]
        halves = [a.astype(BF16) for a in first_powers]
        second_powers = [dot(a, block_diagonal(a, leftb)) for a in halves]
        mixes = [(-0.5625 * a + 0.0625 * b).astype(BF16) for a, b in zip(first_powers, second_powers)]
        zs = [dot(c, block_diagonal(b.astype(BF16), leftb)) for c, b in zip(mixes, second_powers)]
        zs = [
            z + 2.25 * eye - 2.4375 * a + 1.6875 * b
            for z, a, b in zip(zs, first_powers, second_powers)
        ]
        eights = [pl.ds(pl.multiple_of(q * 8, 8), 8) for q in qs]
        sides = [jnp.concatenate([pd[at, :], tails[at, :]], axis=0).astype(BF16) for at in eights]
        products = [dot(p, block_diagonal(z.astype(BF16), leftb)) for p, z in zip(sides, zs)]
        for q, product in zip(qs, products):
            mix = product[0:8]
            pulled = product[8:9] + product[9:10]
            at = pl.ds(pl.multiple_of(q * 8, 8), 8)
            mixed[at, :] = mix
            shift[at, :] = mix * pulled

    shift[...] = half_sums(shift[...])
    one = factors[...]
    root = jnp.sqrt(one)
    one = one * (1.0 / (K - 1))

    def final(pair):
        at = pl.ds(pair, HALF, stride=8)
        return mixed[at, :] * root + shift[at, :] * one

    for pair in range(0, count, 2):
        square = jnp.concatenate([final(pair), final(pair + 1)], axis=0).T
        for which in range(2):
            lag, s = (pair + which) // spec, (pair + which) % spec
            value = packed(square, which == 0) + means[pair + which : pair + which + 1, :]
            out[lag, s] = value.astype(BF16)


def vmem():
    return pl.BlockSpec(memory_space=pltpu.VMEM)


def smem():
    return pl.BlockSpec(memory_space=pltpu.SMEM)


def anywhere():
    return pl.BlockSpec(memory_space=pltpu.HBM)


def stage(prior, coef, column, value, weight, lists, count):
    shapes = [
        jax.ShapeDtypeStruct((1, *prior.shape[1:]), prior.dtype),
        *(jax.ShapeDtypeStruct(x.shape, x.dtype) for x in (coef, column, value, weight, lists)),
        jax.ShapeDtypeStruct((1, 128), jnp.int32),
    ]
    return pl.pallas_call(
        stage_kernel,
        out_shape=shapes,
        in_specs=[anywhere()] * 7,
        out_specs=[vmem()] * 7,
        scratch_shapes=[pltpu.SMEM((1,), jnp.int32), pltpu.SemaphoreType.DMA((7,))],
        compiler_params=pltpu.CompilerParams(vmem_limit_bytes=OBSERVE_BYTES),
        interpret=INTERPRET,
        name="stage",
    )(prior, coef, column, value, weight, lists, count)


def observe(flag, newest, coef, column, value, weight, lists, count):
    slots, halo = column.shape[1], lists.shape[1]
    shapes = [(ROWS, slots), (ROWS, halo), (ROWS, halo)]
    return pl.pallas_call(
        observe_kernel,
        out_shape=[jax.ShapeDtypeStruct(s, BF16) for s in shapes],
        in_specs=[smem()] + [vmem()] * 7,
        out_specs=[vmem()] * 3,
        compiler_params=pltpu.CompilerParams(vmem_limit_bytes=OBSERVE_BYTES),
        interpret=INTERPRET,
        name="observe",
    )(flag, newest, coef, column, value, weight, lists, count)


def prepare(flag, index, local, prior):
    ranks = prior.shape[0] * prior.shape[1]
    shapes = [
        jax.ShapeDtypeStruct((HALF * ranks, 128), F32),
        jax.ShapeDtypeStruct((ranks, 128), F32),
        jax.ShapeDtypeStruct((HALF, 128), F32),
        jax.ShapeDtypeStruct((HALF, 128), F32),
        jax.ShapeDtypeStruct((HALF, 128), jnp.int32),
    ]
    return pl.pallas_call(
        prepare_kernel,
        out_shape=shapes,
        in_specs=[smem()] + [vmem()] * 3,
        out_specs=[vmem()] * 5,
        compiler_params=pltpu.CompilerParams(vmem_limit_bytes=OBSERVE_BYTES),
        interpret=INTERPRET,
        name="prepare",
    )(flag, index, local, prior)


def solve(own, first, second, pd, means, weights, lows, codes, shape):
    return pl.pallas_call(
        solve_kernel,
        out_shape=jax.ShapeDtypeStruct(shape, BF16),
        in_specs=[vmem()] * 8,
        out_specs=vmem(),
        scratch_shapes=[
            pltpu.VMEM((HALF, HALF, 128), F32),
            pltpu.VMEM((HALF, 128), F32),
            pltpu.VMEM((HALF, 128), F32),
            pltpu.VMEM((HALF * 8, 128), F32),
            pltpu.VMEM((HALF * 8, 128), F32),
            pltpu.VMEM((HALF * 8, 128), F32),
        ],
        compiler_params=pltpu.CompilerParams(vmem_limit_bytes=SOLVE_BYTES),
        interpret=INTERPRET,
        name="solve",
    )(own, first, second, pd, means, weights, lows, codes)


def swaps(length, start):
    pairs = []
    for low in range(start, length - 1, 2):
        pairs += [(low, low + 1), (low + 1, low)]
    return pairs


def body(
    prior,
    obs_value,
    obs_weight,
    obs_coef,
    obs_column,
    obs_count,
    halo_lists,
    neighbours,
    localization,
):
    tiles = lax.axis_size("space")
    flag = (lax.axis_index("space") % 2)[None].astype(jnp.int32)
    newest, *staged = stage(
        prior, obs_coef, obs_column[None], obs_value[None], obs_weight[None], halo_lists, obs_count
    )
    newest = lax.all_gather(newest, "lag", axis=0, tiled=True)
    own, first, second = observe(flag, newest, *staged)
    second = lax.ppermute(second, "space", swaps(tiles, 0))
    first = lax.ppermute(first, "space", swaps(tiles, 1))
    ready = prepare(flag, neighbours, localization, prior)
    return solve(own, first, second, *ready, prior.shape)


def solution(mesh):
    return jax.shard_map(
        body,
        mesh=mesh,
        in_specs=(
            P("lag", None, None, "space"),
            P("space"),
            P("space"),
            P(None, "space"),
            P("space"),
            P("space"),
            P(None, "space"),
            P(None, "space"),
            P(None, "space"),
        ),
        out_specs=P("lag", None, None, "space"),
        check_vma=False,
    )
```

```python
import jax
import jax.numpy as jnp
from jax import lax
from jax.experimental import pallas as pl
from jax.experimental.pallas import tpu as pltpu
from jax.sharding import PartitionSpec as P


K = 64
HALF = 64
ROWS = 80
UA = 64
UC = 64
INTERPRET = False
OBSERVE_BYTES = 12 << 20
SOLVE_BYTES = 24 << 20
F32 = jnp.float32
BF16 = jnp.bfloat16


def lanes_of(shape):
    return lax.broadcasted_iota(jnp.int32, shape, len(shape) - 1)


def dot(left, right):
    return jnp.dot(left, right, preferred_element_type=F32)


def stage_kernel(
    prior, coef, column, value, weight, lists,
    newest_out, coef_out, column_out, value_out, weight_out, lists_out,
    sems,
):
    lags = prior.shape[0]
    moves = (
        (prior.at[pl.ds(lags - 1, 1)], newest_out),
        (coef, coef_out),
        (column, column_out),
        (value, value_out),
        (weight, weight_out),
        (lists, lists_out),
    )
    copies = [pltpu.make_async_copy(a, b, sems.at[n]) for n, (a, b) in enumerate(moves)]
    for copy in copies:
        copy.start()
    for copy in copies:
        copy.wait()


def observe_kernel(flag, newest, coef, column, value, weight, lists, count, own, first, second):
    slots = column.shape[1]
    lags, spec = newest.shape[0], newest.shape[1]
    halo = lists.shape[1]
    hot = lax.broadcasted_iota(jnp.int32, (128, slots), 0) == column[...]
    hot = jnp.where(hot, 1.0, 0.0).astype(BF16)
    picked = dot(newest[lags - 1].reshape(spec * K, 128), hot)
    hx = coef[0:1, :] * picked[0:K]
    for s in range(1, spec):
        hx = hx + coef[s : s + 1, :] * picked[s * K : (s + 1) * K]
    mean = jnp.sum(hx, axis=0, keepdims=True) * (1.0 / K)
    valid = jnp.where(lanes_of((1, slots)) < count[:, 0:1], 1.0, 0.0)
    pert = (hx - mean) * valid
    info = jnp.concatenate(
        [weight[...] * valid, (value[...] - mean) * valid, jnp.zeros((ROWS - K - 2, slots), F32)],
        axis=0,
    )
    table = jnp.concatenate([pert, info], axis=0).astype(BF16)
    own[...] = table
    blocks = slots // 128
    stacked = jnp.concatenate([table[:, b * 128 : (b + 1) * 128] for b in range(blocks)], axis=0)
    odd = flag[0] == 1
    for out, mine, other in ((first, 0, 1), (second, 1, 0)):
        index = jnp.where(odd, lists[mine : mine + 1, :], lists[other : other + 1, :])
        low = index & 127
        high = index >> 7
        hot = lax.broadcasted_iota(jnp.int32, (128, halo), 0) == low
        found = dot(stacked, jnp.where(hot, 1.0, 0.0).astype(BF16))
        total = found[0:ROWS]
        for b in range(1, blocks):
            total = jnp.where(high == b, found[b * ROWS : (b + 1) * ROWS], total)
        out[...] = total.astype(BF16)


def packed(square, lower):
    left = lanes_of((HALF, 128)) < HALF
    if lower:
        return jnp.where(left, square[0:HALF], pltpu.roll(square[HALF:], HALF, 1))
    return jnp.where(left, pltpu.roll(square[0:HALF], HALF, 1), square[HALF:])


def block_diagonal(pair, left):
    zero = jnp.zeros_like(pair)
    return jnp.concatenate([jnp.where(left, pair, zero), jnp.where(left, zero, pair)], axis=0)


def prepare_kernel(flag, index, local, prior, pd, means, weights, lows, codes):
    lags, spec = prior.shape[0], prior.shape[1]
    left = lanes_of((HALF, 128)) < HALF

    def beside(values):
        twice = jnp.concatenate([values, values], axis=0).T
        return jnp.where(left, twice[0:HALF], twice[HALF:])

    weights[...] = beside(local[...])
    places = beside(index[...].astype(F32)).astype(jnp.int32)
    block = places >> 8
    lows[...] = (places & 255).astype(F32)
    codes[...] = jnp.where(block >= 4, block ^ (2 * flag[0]), block)

    def rank(pair):
        lag, s = pair // spec, pair % spec
        values = prior[lag, s].astype(F32)
        mean = jnp.sum(values, axis=0, keepdims=True) * (1.0 / K)
        means[pair : pair + 1, :] = mean
        return (values - mean).astype(BF16).astype(F32)

    for pair in range(0, lags * spec, 2):
        square = jnp.concatenate([rank(pair), rank(pair + 1)], axis=0).T
        pd[pl.ds(pair, HALF, stride=8), :] = packed(square, True)
        pd[pl.ds(pair + 1, HALF, stride=8), :] = packed(square, False)


def solve_kernel(
    own, first, second, pd, means, weights, lows, codes, out,
    matrix, squares, factors, tails, mixed, shift,
):
    lags, spec = out.shape[0], out.shape[1]
    count = lags * spec
    halo = first.shape[1]
    left = lanes_of((HALF, 128)) < HALF

    row = lax.broadcasted_iota(jnp.int32, (HALF, 128), 0)
    eye = jnp.where(row == (lanes_of((HALF, 128)) & (HALF - 1)), K - 1.0, 0.0)
    leftb = lanes_of((HALF, 128)) < HALF
    ones = block_diagonal(jnp.ones((HALF, 128), F32), left).astype(BF16)

    sources = [(own, b) for b in range(own.shape[1] // 256)]
    sources += [(ref, b) for ref in (first, second) for b in range(halo // 256)]
    blocks = len(sources)
    views = [ref[:, b * 256 : (b + 1) * 256] for ref, b in sources]
    infos = [view[HALF : HALF + 16].astype(F32) for view in views]
    infos = [info[n : n + 1] for n in range(2) for info in infos]
    stacked = jnp.concatenate(
        [view[0:HALF] for view in views] + [jnp.concatenate(infos, axis=0).astype(BF16)], axis=0
    )
    counts = lax.broadcasted_iota(jnp.int32, (256, 256), 0).astype(F32).astype(BF16)
    which = lax.broadcasted_iota(jnp.int32, (blocks, 256), 0)
    high, none = jnp.ones((256, 256), BF16), jnp.zeros((256, 256), BF16)

    def pick(q):
        low = jnp.concatenate([lows[pl.ds(q, 1), :], lows[pl.ds(q + 1, 1), :]], axis=1)
        code = jnp.concatenate([codes[pl.ds(q, 1), :], codes[pl.ds(q + 1, 1), :]], axis=1)
        found = dot(stacked, jnp.where(counts == low.astype(BF16), high, none))
        total = found[0:HALF]
        for b in range(1, blocks):
            total = jnp.where(code == b, found[b * HALF : (b + 1) * HALF], total)
        mine = which == code
        info = [
            jnp.sum(jnp.where(mine, found[at : at + blocks], 0.0), axis=0, keepdims=True)
            for at in (blocks * HALF, blocks * HALF + blocks)
        ]
        return [
            (total[:, at : at + 128], info[0][:, at : at + 128], info[1][:, at : at + 128])
            for at in (0, 128)
        ]

    @pl.loop(0, HALF // UA)
    def _(step):
        qs = [step * UA + u for u in range(UA)]
        picked = []
        for q in qs[::2]:
            picked += pick(q)
        lefts, diagonals = [], []
        for q, (gathered, info0, info1) in zip(qs, picked):
            scaled = weights[pl.ds(q, 1), :] * info0
            weighted = (gathered * scaled).astype(BF16)
            pull = scaled * info1
            pull_high = pull.astype(BF16).astype(F32)
            extra = jnp.concatenate([pull_high, pull - pull_high, jnp.zeros((14, 128), F32)], axis=0)
            lefts.append(jnp.concatenate([weighted, extra.astype(BF16)], axis=0))
            diagonals.append(block_diagonal(gathered.astype(BF16), leftb))
        products = [
            lax.dot_general(l, d, (((1,), (1,)), ((), ())), preferred_element_type=F32)
            for l, d in zip(lefts, diagonals)
        ]
        for q, product in zip(qs, products):
            full = eye + product[0:HALF]
            matrix[q] = full
            squares[pl.ds(q, 1), :] = jnp.sum(full * full, axis=0, keepdims=True)
            drive = product[HALF : HALF + 1] + product[HALF + 1 : HALF + 2]
            drive_low = drive - drive.astype(BF16).astype(F32)
            tail = jnp.concatenate([drive, drive_low, jnp.zeros((6, 128), F32)], axis=0)
            tails[pl.ds(pl.multiple_of(q * 8, 8), 8), :] = tail

    def half_sums(values):
        high = values.astype(BF16)
        low = (values - high.astype(F32)).astype(BF16)
        return dot(high, ones) + dot(low, ones)

    scale = jnp.sqrt(half_sums(squares[...]))
    factors[...] = 1.0 / scale

    @pl.loop(0, HALF // UC)
    def _(step):
        qs = [step * UC + u for u in range(UC)]
        first_powers = [matrix[q] * factors[pl.ds(q, 1), :] for q in qs]
        halves = [a.astype(BF16) for a in first_powers]
        second_powers = [dot(a, block_diagonal(a, leftb)) for a in halves]
        mixes = [(b - 9.0 * a).astype(BF16) for a, b in zip(first_powers, second_powers)]
        zs = [dot(c, block_diagonal(b.astype(BF16), leftb)) for c, b in zip(mixes, second_powers)]
        zs = [z + 27.0 * b - 39.0 * a for z, a, b in zip(zs, first_powers, second_powers)]
        eights = [pl.ds(pl.multiple_of(q * 8, 8), 8) for q in qs]
        sides = [jnp.concatenate([pd[at, :], tails[at, :]], axis=0).astype(BF16) for at in eights]
        products = [dot(p, block_diagonal(z.astype(BF16), leftb)) for p, z in zip(sides, zs)]
        for at, side, product in zip(eights, sides, products):
            product = product + 36.0 * side.astype(F32)
            mix = product[0:8]
            pulled = product[8:9] + product[9:10]
            mixed[at, :] = mix
            shift[at, :] = mix * pulled

    shift[...] = half_sums(shift[...])
    one = factors[...]
    root = jnp.sqrt(one * (K - 1.0)) * (1.0 / 16.0)
    one = one * (1.0 / 256.0)

    def final(pair):
        at = pl.ds(pair, HALF, stride=8)
        return mixed[at, :] * root + shift[at, :] * one

    for pair in range(0, count, 2):
        square = jnp.concatenate([final(pair), final(pair + 1)], axis=0).T
        for which in range(2):
            lag, s = (pair + which) // spec, (pair + which) % spec
            value = packed(square, which == 0) + means[pair + which : pair + which + 1, :]
            out[lag, s] = value.astype(BF16)


def vmem():
    return pl.BlockSpec(memory_space=pltpu.VMEM)


def smem():
    return pl.BlockSpec(memory_space=pltpu.SMEM)


def anywhere():
    return pl.BlockSpec(memory_space=pltpu.HBM)


def stage(*args):
    prior, *rest = (pltpu.with_memory_space_constraint(x, pltpu.HBM) for x in args)
    shapes = [
        jax.ShapeDtypeStruct((1, *prior.shape[1:]), prior.dtype),
        *(jax.ShapeDtypeStruct(x.shape, x.dtype) for x in rest),
    ]
    return pl.pallas_call(
        stage_kernel,
        out_shape=shapes,
        in_specs=[anywhere()] * 6,
        out_specs=[vmem()] * 6,
        scratch_shapes=[pltpu.SemaphoreType.DMA((6,))],
        compiler_params=pltpu.CompilerParams(vmem_limit_bytes=OBSERVE_BYTES),
        interpret=INTERPRET,
        name="stage",
    )(prior, *rest)


def observe(flag, newest, coef, column, value, weight, lists, count):
    slots, halo = column.shape[1], lists.shape[1]
    shapes = [(ROWS, slots), (ROWS, halo), (ROWS, halo)]
    return pl.pallas_call(
        observe_kernel,
        out_shape=[jax.ShapeDtypeStruct(s, BF16) for s in shapes],
        in_specs=[smem()] + [vmem()] * 7,
        out_specs=[vmem()] * 3,
        compiler_params=pltpu.CompilerParams(vmem_limit_bytes=OBSERVE_BYTES),
        interpret=INTERPRET,
        name="observe",
    )(flag, newest, coef, column, value, weight, lists, count)


def prepare(flag, index, local, prior):
    ranks = prior.shape[0] * prior.shape[1]
    shapes = [
        jax.ShapeDtypeStruct((HALF * ranks, 128), F32),
        jax.ShapeDtypeStruct((ranks, 128), F32),
        jax.ShapeDtypeStruct((HALF, 128), F32),
        jax.ShapeDtypeStruct((HALF, 128), F32),
        jax.ShapeDtypeStruct((HALF, 128), jnp.int32),
    ]
    return pl.pallas_call(
        prepare_kernel,
        out_shape=shapes,
        in_specs=[smem()] + [vmem()] * 3,
        out_specs=[vmem()] * 5,
        compiler_params=pltpu.CompilerParams(vmem_limit_bytes=OBSERVE_BYTES),
        interpret=INTERPRET,
        name="prepare",
    )(flag, index, local, prior)


def solve(own, first, second, pd, means, weights, lows, codes, shape):
    return pl.pallas_call(
        solve_kernel,
        out_shape=jax.ShapeDtypeStruct(shape, BF16),
        in_specs=[vmem()] * 8,
        out_specs=vmem(),
        scratch_shapes=[
            pltpu.VMEM((HALF, HALF, 128), F32),
            pltpu.VMEM((HALF, 128), F32),
            pltpu.VMEM((HALF, 128), F32),
            pltpu.VMEM((HALF * 8, 128), F32),
            pltpu.VMEM((HALF * 8, 128), F32),
            pltpu.VMEM((HALF * 8, 128), F32),
        ],
        compiler_params=pltpu.CompilerParams(vmem_limit_bytes=SOLVE_BYTES),
        interpret=INTERPRET,
        name="solve",
    )(own, first, second, pd, means, weights, lows, codes)


def swaps(length, start):
    pairs = []
    for low in range(start, length - 1, 2):
        pairs += [(low, low + 1), (low + 1, low)]
    return pairs


def body(
    prior,
    obs_value,
    obs_weight,
    obs_coef,
    obs_column,
    obs_count,
    halo_lists,
    neighbours,
    localization,
):
    tiles = lax.axis_size("space")
    flag = (lax.axis_index("space") % 2)[None].astype(jnp.int32)
    newest, *staged = stage(
        prior, obs_coef, obs_column[None], obs_value[None], obs_weight[None], halo_lists
    )
    newest = lax.all_gather(newest, "lag", axis=0, tiled=True)
    own, first, second = observe(flag, newest, *staged, obs_count[None])
    second = lax.ppermute(second, "space", swaps(tiles, 0))
    first = lax.ppermute(first, "space", swaps(tiles, 1))
    ready = prepare(flag, neighbours, localization, prior)
    return solve(own, first, second, *ready, prior.shape)


def solution(mesh):
    return jax.shard_map(
        body,
        mesh=mesh,
        in_specs=(
            P("lag", None, None, "space"),
            P("space"),
            P("space"),
            P(None, "space"),
            P("space"),
            P("space"),
            P(None, "space"),
            P(None, "space"),
            P(None, "space"),
        ),
        out_specs=P("lag", None, None, "space"),
        check_vma=False,
    )
```

```python
import jax
import jax.numpy as jnp
from jax import lax
from jax.experimental import pallas as pl
from jax.experimental.pallas import tpu as pltpu
from jax.sharding import PartitionSpec as P


K = 64
HALF = 64
ROWS = 80
UE = 64
UA = 64
UC = 64
INTERPRET = False
OBSERVE_BYTES = 12 << 20
SOLVE_BYTES = 24 << 20
F32 = jnp.float32
BF16 = jnp.bfloat16


def lanes_of(shape):
    return lax.broadcasted_iota(jnp.int32, shape, len(shape) - 1)


def dot(left, right):
    return jnp.dot(left, right, preferred_element_type=F32)


def stage_kernel(
    prior, coef, column, value, weight, lists,
    newest_out, coef_out, column_out, value_out, weight_out, lists_out,
    sems,
):
    lags = prior.shape[0]
    moves = (
        (prior.at[pl.ds(lags - 1, 1)], newest_out),
        (coef, coef_out),
        (column, column_out),
        (value, value_out),
        (weight, weight_out),
        (lists, lists_out),
    )
    copies = [pltpu.make_async_copy(a, b, sems.at[n]) for n, (a, b) in enumerate(moves)]
    for copy in copies:
        copy.start()
    for copy in copies:
        copy.wait()


def observe_kernel(flag, newest, coef, column, value, weight, lists, count, own, first, second):
    slots = column.shape[1]
    lags, spec = newest.shape[0], newest.shape[1]
    halo = lists.shape[1]
    hot = lax.broadcasted_iota(jnp.int32, (128, slots), 0) == column[...]
    hot = jnp.where(hot, 1.0, 0.0).astype(BF16)
    picked = dot(newest[lags - 1].reshape(spec * K, 128), hot)
    hx = coef[0:1, :] * picked[0:K]
    for s in range(1, spec):
        hx = hx + coef[s : s + 1, :] * picked[s * K : (s + 1) * K]
    mean = jnp.sum(hx, axis=0, keepdims=True) * (1.0 / K)
    valid = jnp.where(lanes_of((1, slots)) < count[:, 0:1], 1.0, 0.0)
    pert = (hx - mean) * valid
    info = jnp.concatenate(
        [weight[...] * valid, (value[...] - mean) * valid, jnp.zeros((ROWS - K - 2, slots), F32)],
        axis=0,
    )
    table = jnp.concatenate([pert, info], axis=0).astype(BF16)
    own[...] = table
    blocks = slots // 128
    stacked = jnp.concatenate([table[:, b * 128 : (b + 1) * 128] for b in range(blocks)], axis=0)
    odd = flag[0] == 1
    for out, mine, other in ((first, 0, 1), (second, 1, 0)):
        index = jnp.where(odd, lists[mine : mine + 1, :], lists[other : other + 1, :])
        low = index & 127
        high = index >> 7
        hot = lax.broadcasted_iota(jnp.int32, (128, halo), 0) == low
        found = dot(stacked, jnp.where(hot, 1.0, 0.0).astype(BF16))
        total = found[0:ROWS]
        for b in range(1, blocks):
            total = jnp.where(high == b, found[b * ROWS : (b + 1) * ROWS], total)
        out[...] = total.astype(BF16)


def packed(square, lower):
    left = lanes_of((HALF, 128)) < HALF
    if lower:
        return jnp.where(left, square[0:HALF], pltpu.roll(square[HALF:], HALF, 1))
    return jnp.where(left, pltpu.roll(square[0:HALF], HALF, 1), square[HALF:])


def block_diagonal(pair, left):
    zero = jnp.zeros_like(pair)
    return jnp.concatenate([jnp.where(left, pair, zero), jnp.where(left, zero, pair)], axis=0)


def prepare_kernel(flag, index, local, prior, pd, means, weights, lows, codes):
    lags, spec = prior.shape[0], prior.shape[1]
    left = lanes_of((HALF, 128)) < HALF

    def beside(values):
        twice = jnp.concatenate([values, values], axis=0).T
        return jnp.where(left, twice[0:HALF], twice[HALF:])

    weights[...] = beside(local[...])
    places = beside(index[...].astype(F32)).astype(jnp.int32)
    block = places >> 8
    lows[...] = (places & 255).astype(F32)
    codes[...] = jnp.where(block >= 4, block ^ (2 * flag[0]), block)

    def rank(pair):
        lag, s = pair // spec, pair % spec
        values = prior[lag, s].astype(F32)
        mean = jnp.sum(values, axis=0, keepdims=True) * (1.0 / K)
        means[pair : pair + 1, :] = mean
        return (values - mean).astype(BF16).astype(F32)

    for pair in range(0, lags * spec, 2):
        square = jnp.concatenate([rank(pair), rank(pair + 1)], axis=0).T
        pd[pl.ds(pair, HALF, stride=8), :] = packed(square, True)
        pd[pl.ds(pair + 1, HALF, stride=8), :] = packed(square, False)


def gatherer(sources, codes_of, lows, codes):
    blocks = 8
    views = dict(zip(codes_of, (ref[:, b * 256 : (b + 1) * 256] for ref, b in sources)))
    zero = jnp.zeros((16, 256), F32)
    infos = [views[b][HALF : HALF + 16].astype(F32) if b in views else zero for b in range(blocks)]
    infos = [info[n : n + 1] for n in range(2) for info in infos]
    stacked = jnp.concatenate(
        [views[b][0:HALF] for b in codes_of] + [jnp.concatenate(infos, axis=0).astype(BF16)], axis=0
    )
    counts = lax.broadcasted_iota(jnp.int32, (256, 256), 0).astype(F32).astype(BF16)
    which = lax.broadcasted_iota(jnp.int32, (blocks, 256), 0)
    high, none = jnp.ones((256, 256), BF16), jnp.zeros((256, 256), BF16)
    tail = len(codes_of) * HALF

    def pick(q, total):
        low = jnp.concatenate([lows[pl.ds(q, 1), :], lows[pl.ds(q + 1, 1), :]], axis=1)
        code = jnp.concatenate([codes[pl.ds(q, 1), :], codes[pl.ds(q + 1, 1), :]], axis=1)
        found = dot(stacked, jnp.where(counts == low.astype(BF16), high, none))
        for n, b in enumerate(codes_of):
            part = found[n * HALF : (n + 1) * HALF]
            total = part if total is None else jnp.where(code == b, part, total)
        mine = which == code
        info = [
            jnp.sum(jnp.where(mine, found[at : at + blocks], 0.0), axis=0, keepdims=True)
            for at in (tail, tail + blocks)
        ]
        return [
            (total[:, at : at + 128], info[0][:, at : at + 128], info[1][:, at : at + 128])
            for at in (0, 128)
        ]

    return pick


def early_kernel(own, second, lows, codes, partial, info0_out, info1_out):
    pick = gatherer(
        [(own, b) for b in range(4)] + [(second, b) for b in range(2)],
        (0, 1, 2, 3, 6, 7), lows, codes,
    )

    @pl.loop(0, HALF // UE)
    def _(step):
        for u in range(0, UE, 2):
            q = step * UE + u
            for n, (total, info0, info1) in enumerate(pick(q, None)):
                partial[q + n] = total
                info0_out[pl.ds(q + n, 1), :] = info0
                info1_out[pl.ds(q + n, 1), :] = info1


def solve_kernel(
    first, partial, early0, early1, pd, means, weights, lows, codes, out,
    matrix, squares, factors, tails, mixed, shift,
):
    lags, spec = out.shape[0], out.shape[1]
    count = lags * spec
    left = lanes_of((HALF, 128)) < HALF
    row = lax.broadcasted_iota(jnp.int32, (HALF, 128), 0)
    eye = jnp.where(row == (lanes_of((HALF, 128)) & (HALF - 1)), K - 1.0, 0.0)
    leftb = lanes_of((HALF, 128)) < HALF
    ones = block_diagonal(jnp.ones((HALF, 128), F32), left).astype(BF16)
    pick = gatherer([(first, b) for b in range(2)], (4, 5), lows, codes)

    @pl.loop(0, HALF // UA)
    def _(step):
        qs = [step * UA + u for u in range(UA)]
        picked = []
        for q in qs[::2]:
            picked += pick(q, jnp.concatenate([partial[q], partial[q + 1]], axis=1))
        lefts, diagonals = [], []
        for q, (gathered, info0, info1) in zip(qs, picked):
            info0 = info0 + early0[pl.ds(q, 1), :]
            info1 = info1 + early1[pl.ds(q, 1), :]
            scaled = weights[pl.ds(q, 1), :] * info0
            weighted = (gathered * scaled).astype(BF16)
            pull = scaled * info1
            pull_high = pull.astype(BF16).astype(F32)
            extra = jnp.concatenate([pull_high, pull - pull_high, jnp.zeros((14, 128), F32)], axis=0)
            lefts.append(jnp.concatenate([weighted, extra.astype(BF16)], axis=0))
            diagonals.append(block_diagonal(gathered.astype(BF16), leftb))
        products = [
            lax.dot_general(l, d, (((1,), (1,)), ((), ())), preferred_element_type=F32)
            for l, d in zip(lefts, diagonals)
        ]
        for q, product in zip(qs, products):
            full = eye + product[0:HALF]
            matrix[q] = full
            squares[pl.ds(q, 1), :] = jnp.sum(full * full, axis=0, keepdims=True)
            drive = product[HALF : HALF + 1] + product[HALF + 1 : HALF + 2]
            drive_low = drive - drive.astype(BF16).astype(F32)
            tail = jnp.concatenate([drive, drive_low, jnp.zeros((6, 128), F32)], axis=0)
            tails[pl.ds(pl.multiple_of(q * 8, 8), 8), :] = tail

    def half_sums(values):
        high = values.astype(BF16)
        low = (values - high.astype(F32)).astype(BF16)
        return dot(high, ones) + dot(low, ones)

    scale = jnp.sqrt(half_sums(squares[...]))
    factors[...] = 1.0 / scale

    @pl.loop(0, HALF // UC)
    def _(step):
        qs = [step * UC + u for u in range(UC)]
        first_powers = [matrix[q] * factors[pl.ds(q, 1), :] for q in qs]
        halves = [a.astype(BF16) for a in first_powers]
        second_powers = [dot(a, block_diagonal(a, leftb)) for a in halves]
        mixes = [(b - 9.0 * a).astype(BF16) for a, b in zip(first_powers, second_powers)]
        zs = [dot(c, block_diagonal(b.astype(BF16), leftb)) for c, b in zip(mixes, second_powers)]
        zs = [z + 27.0 * b - 39.0 * a for z, a, b in zip(zs, first_powers, second_powers)]
        eights = [pl.ds(pl.multiple_of(q * 8, 8), 8) for q in qs]
        sides = [jnp.concatenate([pd[at, :], tails[at, :]], axis=0).astype(BF16) for at in eights]
        products = [dot(p, block_diagonal(z.astype(BF16), leftb)) for p, z in zip(sides, zs)]
        for at, side, product in zip(eights, sides, products):
            product = product + 36.0 * side.astype(F32)
            mix = product[0:8]
            pulled = product[8:9] + product[9:10]
            mixed[at, :] = mix
            shift[at, :] = mix * pulled

    shift[...] = half_sums(shift[...])
    one = factors[...]
    root = jnp.sqrt(one * (K - 1.0)) * (1.0 / 16.0)
    one = one * (1.0 / 256.0)

    def final(pair):
        at = pl.ds(pair, HALF, stride=8)
        return mixed[at, :] * root + shift[at, :] * one

    for pair in range(0, count, 2):
        square = jnp.concatenate([final(pair), final(pair + 1)], axis=0).T
        for which in range(2):
            lag, s = (pair + which) // spec, (pair + which) % spec
            value = packed(square, which == 0) + means[pair + which : pair + which + 1, :]
            out[lag, s] = value.astype(BF16)


def vmem():
    return pl.BlockSpec(memory_space=pltpu.VMEM)


def smem():
    return pl.BlockSpec(memory_space=pltpu.SMEM)


def anywhere():
    return pl.BlockSpec(memory_space=pltpu.HBM)


def stage(*args):
    prior, *rest = (pltpu.with_memory_space_constraint(x, pltpu.HBM) for x in args)
    shapes = [
        jax.ShapeDtypeStruct((1, *prior.shape[1:]), prior.dtype),
        *(jax.ShapeDtypeStruct(x.shape, x.dtype) for x in rest),
    ]
    return pl.pallas_call(
        stage_kernel,
        out_shape=shapes,
        in_specs=[anywhere()] * 6,
        out_specs=[vmem()] * 6,
        scratch_shapes=[pltpu.SemaphoreType.DMA((6,))],
        compiler_params=pltpu.CompilerParams(vmem_limit_bytes=OBSERVE_BYTES),
        interpret=INTERPRET,
        name="stage",
    )(prior, *rest)


def observe(flag, newest, coef, column, value, weight, lists, count):
    slots, halo = column.shape[1], lists.shape[1]
    shapes = [(ROWS, slots), (ROWS, halo), (ROWS, halo)]
    return pl.pallas_call(
        observe_kernel,
        out_shape=[jax.ShapeDtypeStruct(s, BF16) for s in shapes],
        in_specs=[smem()] + [vmem()] * 7,
        out_specs=[vmem()] * 3,
        compiler_params=pltpu.CompilerParams(vmem_limit_bytes=OBSERVE_BYTES),
        interpret=INTERPRET,
        name="observe",
    )(flag, newest, coef, column, value, weight, lists, count)


def prepare(flag, index, local, prior):
    ranks = prior.shape[0] * prior.shape[1]
    shapes = [
        jax.ShapeDtypeStruct((HALF * ranks, 128), F32),
        jax.ShapeDtypeStruct((ranks, 128), F32),
        jax.ShapeDtypeStruct((HALF, 128), F32),
        jax.ShapeDtypeStruct((HALF, 128), F32),
        jax.ShapeDtypeStruct((HALF, 128), jnp.int32),
    ]
    return pl.pallas_call(
        prepare_kernel,
        out_shape=shapes,
        in_specs=[smem()] + [vmem()] * 3,
        out_specs=[vmem()] * 5,
        compiler_params=pltpu.CompilerParams(vmem_limit_bytes=OBSERVE_BYTES),
        interpret=INTERPRET,
        name="prepare",
    )(flag, index, local, prior)


def early(own, second, lows, codes):
    shapes = [(HALF, HALF, 128), (HALF, 128), (HALF, 128)]
    return pl.pallas_call(
        early_kernel,
        out_shape=[jax.ShapeDtypeStruct(x, F32) for x in shapes],
        in_specs=[vmem()] * 4,
        out_specs=[vmem()] * 3,
        compiler_params=pltpu.CompilerParams(vmem_limit_bytes=SOLVE_BYTES),
        interpret=INTERPRET,
        name="early",
    )(own, second, lows, codes)


def solve(own, first, second, pd, means, weights, lows, codes, shape):
    partial = early(own, second, lows, codes)
    return pl.pallas_call(
        solve_kernel,
        out_shape=jax.ShapeDtypeStruct(shape, BF16),
        in_specs=[vmem()] * 9,
        out_specs=vmem(),
        scratch_shapes=[
            pltpu.VMEM((HALF, HALF, 128), F32),
            pltpu.VMEM((HALF, 128), F32),
            pltpu.VMEM((HALF, 128), F32),
            pltpu.VMEM((HALF * 8, 128), F32),
            pltpu.VMEM((HALF * 8, 128), F32),
            pltpu.VMEM((HALF * 8, 128), F32),
        ],
        compiler_params=pltpu.CompilerParams(vmem_limit_bytes=SOLVE_BYTES),
        interpret=INTERPRET,
        name="solve",
    )(first, *partial, pd, means, weights, lows, codes)


def swaps(length, start):
    pairs = []
    for low in range(start, length - 1, 2):
        pairs += [(low, low + 1), (low + 1, low)]
    return pairs


def body(
    prior,
    obs_value,
    obs_weight,
    obs_coef,
    obs_column,
    obs_count,
    halo_lists,
    neighbours,
    localization,
):
    tiles = lax.axis_size("space")
    flag = (lax.axis_index("space") % 2)[None].astype(jnp.int32)
    newest, *staged = stage(
        prior, obs_coef, obs_column[None], obs_value[None], obs_weight[None], halo_lists
    )
    newest = lax.all_gather(newest, "lag", axis=0, tiled=True)
    own, first, second = observe(flag, newest, *staged, obs_count[None])
    second = lax.ppermute(second, "space", swaps(tiles, 0))
    first = lax.ppermute(first, "space", swaps(tiles, 1))
    ready = prepare(flag, neighbours, localization, prior)
    return solve(own, first, second, *ready, prior.shape)


def solution(mesh):
    return jax.shard_map(
        body,
        mesh=mesh,
        in_specs=(
            P("lag", None, None, "space"),
            P("space"),
            P("space"),
            P(None, "space"),
            P("space"),
            P("space"),
            P(None, "space"),
            P(None, "space"),
            P(None, "space"),
        ),
        out_specs=P("lag", None, None, "space"),
        check_vma=False,
    )
```

```python
import jax
import jax.numpy as jnp
from jax import lax
from jax.experimental import pallas as pl
from jax.experimental.pallas import tpu as pltpu
from jax.sharding import PartitionSpec as P


K = 64
HALF = 64
ROWS = 80
UE = 64
UA = 64
UC = 64
INTERPRET = False
OBSERVE_BYTES = 12 << 20
SOLVE_BYTES = 24 << 20
F32 = jnp.float32
BF16 = jnp.bfloat16


def lanes_of(shape):
    return lax.broadcasted_iota(jnp.int32, shape, len(shape) - 1)


def dot(left, right):
    return jnp.dot(left, right, preferred_element_type=F32)


def stage_kernel(
    prior, coef, column, value, weight, lists,
    newest_out, coef_out, column_out, value_out, weight_out, lists_out,
    sems,
):
    lags = prior.shape[0]
    moves = (
        (prior.at[pl.ds(lags - 1, 1)], newest_out),
        (coef, coef_out),
        (column, column_out),
        (value, value_out),
        (weight, weight_out),
        (lists, lists_out),
    )
    copies = [pltpu.make_async_copy(a, b, sems.at[n]) for n, (a, b) in enumerate(moves)]
    for copy in copies:
        copy.start()
    for copy in copies:
        copy.wait()


def observe_kernel(
    flag, newest, coef, column, value, weight, lists, count, prior, index, local,
    own, first, second, prior_out, index_out, local_out, sems,
):
    moves = ((prior, prior_out), (index, index_out), (local, local_out))
    copies = [pltpu.make_async_copy(a, b, sems.at[n]) for n, (a, b) in enumerate(moves)]
    for copy in copies:
        copy.start()
    slots = column.shape[1]
    lags, spec = newest.shape[0], newest.shape[1]
    halo = lists.shape[1]
    hot = lax.broadcasted_iota(jnp.int32, (128, slots), 0) == column[...]
    hot = jnp.where(hot, 1.0, 0.0).astype(BF16)
    picked = dot(newest[lags - 1].reshape(spec * K, 128), hot)
    hx = coef[0:1, :] * picked[0:K]
    for s in range(1, spec):
        hx = hx + coef[s : s + 1, :] * picked[s * K : (s + 1) * K]
    mean = jnp.sum(hx, axis=0, keepdims=True) * (1.0 / K)
    valid = jnp.where(lanes_of((1, slots)) < count[:, 0:1], 1.0, 0.0)
    pert = (hx - mean) * valid
    info = jnp.concatenate(
        [weight[...] * valid, (value[...] - mean) * valid, jnp.zeros((ROWS - K - 2, slots), F32)],
        axis=0,
    )
    table = jnp.concatenate([pert, info], axis=0).astype(BF16)
    own[...] = table
    blocks = slots // 128
    stacked = jnp.concatenate([table[:, b * 128 : (b + 1) * 128] for b in range(blocks)], axis=0)
    odd = flag[0] == 1
    for out, mine, other in ((first, 0, 1), (second, 1, 0)):
        index = jnp.where(odd, lists[mine : mine + 1, :], lists[other : other + 1, :])
        low = index & 127
        high = index >> 7
        hot = lax.broadcasted_iota(jnp.int32, (128, halo), 0) == low
        found = dot(stacked, jnp.where(hot, 1.0, 0.0).astype(BF16))
        total = found[0:ROWS]
        for b in range(1, blocks):
            total = jnp.where(high == b, found[b * ROWS : (b + 1) * ROWS], total)
        out[...] = total.astype(BF16)
    for copy in copies:
        copy.wait()


def packed(square, lower):
    left = lanes_of((HALF, 128)) < HALF
    if lower:
        return jnp.where(left, square[0:HALF], pltpu.roll(square[HALF:], HALF, 1))
    return jnp.where(left, pltpu.roll(square[0:HALF], HALF, 1), square[HALF:])


def block_diagonal(pair, left):
    zero = jnp.zeros_like(pair)
    return jnp.concatenate([jnp.where(left, pair, zero), jnp.where(left, zero, pair)], axis=0)


def prepare_kernel(flag, index, local, prior, pd, means, weights, lows, codes):
    lags, spec = prior.shape[0], prior.shape[1]
    left = lanes_of((HALF, 128)) < HALF

    def beside(values):
        twice = jnp.concatenate([values, values], axis=0).T
        return jnp.where(left, twice[0:HALF], twice[HALF:])

    weights[...] = beside(local[...])
    places = beside(index[...].astype(F32)).astype(jnp.int32)
    block = places >> 8
    lows[...] = (places & 255).astype(F32)
    codes[...] = jnp.where(block >= 4, block ^ (2 * flag[0]), block)

    def rank(pair):
        lag, s = pair // spec, pair % spec
        values = prior[lag, s].astype(F32)
        mean = jnp.sum(values, axis=0, keepdims=True) * (1.0 / K)
        means[pair : pair + 1, :] = mean
        return (values - mean).astype(BF16).astype(F32)

    for pair in range(0, lags * spec, 2):
        square = jnp.concatenate([rank(pair), rank(pair + 1)], axis=0).T
        pd[pl.ds(pair, HALF, stride=8), :] = packed(square, True)
        pd[pl.ds(pair + 1, HALF, stride=8), :] = packed(square, False)


def gatherer(sources, codes_of, lows, codes):
    blocks = 8
    views = dict(zip(codes_of, (ref[:, b * 256 : (b + 1) * 256] for ref, b in sources)))
    zero = jnp.zeros((16, 256), F32)
    infos = [views[b][HALF : HALF + 16].astype(F32) if b in views else zero for b in range(blocks)]
    infos = [info[n : n + 1] for n in range(2) for info in infos]
    stacked = jnp.concatenate(
        [views[b][0:HALF] for b in codes_of] + [jnp.concatenate(infos, axis=0).astype(BF16)], axis=0
    )
    counts = lax.broadcasted_iota(jnp.int32, (256, 256), 0).astype(F32).astype(BF16)
    which = lax.broadcasted_iota(jnp.int32, (blocks, 256), 0)
    high, none = jnp.ones((256, 256), BF16), jnp.zeros((256, 256), BF16)
    tail = len(codes_of) * HALF

    def pick(q, total):
        low = jnp.concatenate([lows[pl.ds(q, 1), :], lows[pl.ds(q + 1, 1), :]], axis=1)
        code = jnp.concatenate([codes[pl.ds(q, 1), :], codes[pl.ds(q + 1, 1), :]], axis=1)
        found = dot(stacked, jnp.where(counts == low.astype(BF16), high, none))
        for n, b in enumerate(codes_of):
            part = found[n * HALF : (n + 1) * HALF]
            total = part if total is None else jnp.where(code == b, part, total)
        mine = which == code
        info = [
            jnp.sum(jnp.where(mine, found[at : at + blocks], 0.0), axis=0, keepdims=True)
            for at in (tail, tail + blocks)
        ]
        return [
            (total[:, at : at + 128], info[0][:, at : at + 128], info[1][:, at : at + 128])
            for at in (0, 128)
        ]

    return pick


def early_kernel(own, second, lows, codes, partial, info0_out, info1_out):
    pick = gatherer(
        [(own, b) for b in range(4)] + [(second, b) for b in range(2)],
        (0, 1, 2, 3, 6, 7), lows, codes,
    )

    @pl.loop(0, HALF // UE)
    def _(step):
        for u in range(0, UE, 2):
            q = step * UE + u
            for n, (total, info0, info1) in enumerate(pick(q, None)):
                partial[q + n] = total
                info0_out[pl.ds(q + n, 1), :] = info0
                info1_out[pl.ds(q + n, 1), :] = info1


def solve_kernel(
    first, partial, early0, early1, pd, means, weights, lows, codes, out,
    matrix, squares, factors, tails, mixed, shift,
):
    lags, spec = out.shape[0], out.shape[1]
    count = lags * spec
    left = lanes_of((HALF, 128)) < HALF
    row = lax.broadcasted_iota(jnp.int32, (HALF, 128), 0)
    eye = jnp.where(row == (lanes_of((HALF, 128)) & (HALF - 1)), K - 1.0, 0.0)
    leftb = lanes_of((HALF, 128)) < HALF
    ones = block_diagonal(jnp.ones((HALF, 128), F32), left).astype(BF16)
    pick = gatherer([(first, b) for b in range(2)], (4, 5), lows, codes)

    @pl.loop(0, HALF // UA)
    def _(step):
        qs = [step * UA + u for u in range(UA)]
        picked = []
        for q in qs[::2]:
            picked += pick(q, jnp.concatenate([partial[q], partial[q + 1]], axis=1))
        lefts, diagonals = [], []
        for q, (gathered, info0, info1) in zip(qs, picked):
            info0 = info0 + early0[pl.ds(q, 1), :]
            info1 = info1 + early1[pl.ds(q, 1), :]
            scaled = weights[pl.ds(q, 1), :] * info0
            weighted = (gathered * scaled).astype(BF16)
            pull = scaled * info1
            pull_high = pull.astype(BF16).astype(F32)
            extra = jnp.concatenate([pull_high, pull - pull_high, jnp.zeros((14, 128), F32)], axis=0)
            lefts.append(jnp.concatenate([weighted, extra.astype(BF16)], axis=0))
            diagonals.append(block_diagonal(gathered.astype(BF16), leftb))
        products = [
            lax.dot_general(l, d, (((1,), (1,)), ((), ())), preferred_element_type=F32)
            for l, d in zip(lefts, diagonals)
        ]
        for q, product in zip(qs, products):
            full = eye + product[0:HALF]
            matrix[q] = full
            squares[pl.ds(q, 1), :] = jnp.sum(full * full, axis=0, keepdims=True)
            drive = product[HALF : HALF + 1] + product[HALF + 1 : HALF + 2]
            drive_low = drive - drive.astype(BF16).astype(F32)
            tail = jnp.concatenate([drive, drive_low, jnp.zeros((6, 128), F32)], axis=0)
            tails[pl.ds(pl.multiple_of(q * 8, 8), 8), :] = tail

    def half_sums(values):
        high = values.astype(BF16)
        low = (values - high.astype(F32)).astype(BF16)
        return dot(high, ones) + dot(low, ones)

    scale = jnp.sqrt(half_sums(squares[...]))
    factors[...] = 1.0 / scale

    @pl.loop(0, HALF // UC)
    def _(step):
        qs = [step * UC + u for u in range(UC)]
        first_powers = [matrix[q] * factors[pl.ds(q, 1), :] for q in qs]
        halves = [a.astype(BF16) for a in first_powers]
        second_powers = [dot(a, block_diagonal(a, leftb)) for a in halves]
        mixes = [(b - 9.0 * a).astype(BF16) for a, b in zip(first_powers, second_powers)]
        zs = [dot(c, block_diagonal(b.astype(BF16), leftb)) for c, b in zip(mixes, second_powers)]
        zs = [z + 27.0 * b - 39.0 * a for z, a, b in zip(zs, first_powers, second_powers)]
        eights = [pl.ds(pl.multiple_of(q * 8, 8), 8) for q in qs]
        sides = [jnp.concatenate([pd[at, :], tails[at, :]], axis=0).astype(BF16) for at in eights]
        products = [dot(p, block_diagonal(z.astype(BF16), leftb)) for p, z in zip(sides, zs)]
        for at, side, product in zip(eights, sides, products):
            product = product + 36.0 * side.astype(F32)
            mix = product[0:8]
            pulled = product[8:9] + product[9:10]
            mixed[at, :] = mix
            shift[at, :] = mix * pulled

    shift[...] = half_sums(shift[...])
    one = factors[...]
    root = jnp.sqrt(one * (K - 1.0)) * (1.0 / 16.0)
    one = one * (1.0 / 256.0)

    def final(pair):
        at = pl.ds(pair, HALF, stride=8)
        return mixed[at, :] * root + shift[at, :] * one

    for pair in range(0, count, 2):
        square = jnp.concatenate([final(pair), final(pair + 1)], axis=0).T
        for which in range(2):
            lag, s = (pair + which) // spec, (pair + which) % spec
            value = packed(square, which == 0) + means[pair + which : pair + which + 1, :]
            out[lag, s] = value.astype(BF16)


def vmem():
    return pl.BlockSpec(memory_space=pltpu.VMEM)


def smem():
    return pl.BlockSpec(memory_space=pltpu.SMEM)


def anywhere():
    return pl.BlockSpec(memory_space=pltpu.HBM)


def stage(*args):
    prior, *rest = (pltpu.with_memory_space_constraint(x, pltpu.HBM) for x in args)
    shapes = [
        jax.ShapeDtypeStruct((1, *prior.shape[1:]), prior.dtype),
        *(jax.ShapeDtypeStruct(x.shape, x.dtype) for x in rest),
    ]
    return pl.pallas_call(
        stage_kernel,
        out_shape=shapes,
        in_specs=[anywhere()] * 6,
        out_specs=[vmem()] * 6,
        scratch_shapes=[pltpu.SemaphoreType.DMA((6,))],
        compiler_params=pltpu.CompilerParams(vmem_limit_bytes=OBSERVE_BYTES),
        interpret=INTERPRET,
        name="stage",
    )(prior, *rest)


def observe(flag, newest, coef, column, value, weight, lists, count, *later):
    slots, halo = column.shape[1], lists.shape[1]
    shapes = [(ROWS, slots), (ROWS, halo), (ROWS, halo)]
    later = [pltpu.with_memory_space_constraint(x, pltpu.HBM) for x in later]
    return pl.pallas_call(
        observe_kernel,
        out_shape=[jax.ShapeDtypeStruct(s, BF16) for s in shapes]
        + [jax.ShapeDtypeStruct(x.shape, x.dtype) for x in later],
        in_specs=[smem()] + [vmem()] * 7 + [anywhere()] * 3,
        out_specs=[vmem()] * 6,
        scratch_shapes=[pltpu.SemaphoreType.DMA((3,))],
        compiler_params=pltpu.CompilerParams(vmem_limit_bytes=OBSERVE_BYTES),
        interpret=INTERPRET,
        name="observe",
    )(flag, newest, coef, column, value, weight, lists, count, *later)


def prepare(flag, index, local, prior):
    ranks = prior.shape[0] * prior.shape[1]
    shapes = [
        jax.ShapeDtypeStruct((HALF * ranks, 128), F32),
        jax.ShapeDtypeStruct((ranks, 128), F32),
        jax.ShapeDtypeStruct((HALF, 128), F32),
        jax.ShapeDtypeStruct((HALF, 128), F32),
        jax.ShapeDtypeStruct((HALF, 128), jnp.int32),
    ]
    return pl.pallas_call(
        prepare_kernel,
        out_shape=shapes,
        in_specs=[smem()] + [vmem()] * 3,
        out_specs=[vmem()] * 5,
        compiler_params=pltpu.CompilerParams(vmem_limit_bytes=OBSERVE_BYTES),
        interpret=INTERPRET,
        name="prepare",
    )(flag, index, local, prior)


def early(own, second, lows, codes):
    shapes = [(HALF, HALF, 128), (HALF, 128), (HALF, 128)]
    return pl.pallas_call(
        early_kernel,
        out_shape=[jax.ShapeDtypeStruct(x, F32) for x in shapes],
        in_specs=[vmem()] * 4,
        out_specs=[vmem()] * 3,
        compiler_params=pltpu.CompilerParams(vmem_limit_bytes=SOLVE_BYTES),
        interpret=INTERPRET,
        name="early",
    )(own, second, lows, codes)


def solve(own, first, second, pd, means, weights, lows, codes, shape):
    partial = early(own, second, lows, codes)
    return pl.pallas_call(
        solve_kernel,
        out_shape=jax.ShapeDtypeStruct(shape, BF16),
        in_specs=[vmem()] * 9,
        out_specs=vmem(),
        scratch_shapes=[
            pltpu.VMEM((HALF, HALF, 128), F32),
            pltpu.VMEM((HALF, 128), F32),
            pltpu.VMEM((HALF, 128), F32),
            pltpu.VMEM((HALF * 8, 128), F32),
            pltpu.VMEM((HALF * 8, 128), F32),
            pltpu.VMEM((HALF * 8, 128), F32),
        ],
        compiler_params=pltpu.CompilerParams(vmem_limit_bytes=SOLVE_BYTES),
        interpret=INTERPRET,
        name="solve",
    )(first, *partial, pd, means, weights, lows, codes)


def swaps(length, start):
    pairs = []
    for low in range(start, length - 1, 2):
        pairs += [(low, low + 1), (low + 1, low)]
    return pairs


def body(
    prior,
    obs_value,
    obs_weight,
    obs_coef,
    obs_column,
    obs_count,
    halo_lists,
    neighbours,
    localization,
):
    tiles = lax.axis_size("space")
    flag = (lax.axis_index("space") % 2)[None].astype(jnp.int32)
    newest, *staged = stage(
        prior, obs_coef, obs_column[None], obs_value[None], obs_weight[None], halo_lists
    )
    newest = lax.all_gather(newest, "lag", axis=0, tiled=True)
    own, first, second, prior, index, local = observe(
        flag, newest, *staged, obs_count[None], prior, neighbours, localization
    )
    second = lax.ppermute(second, "space", swaps(tiles, 0))
    first = lax.ppermute(first, "space", swaps(tiles, 1))
    ready = prepare(flag, index, local, prior)
    return solve(own, first, second, *ready, prior.shape)


def solution(mesh):
    return jax.shard_map(
        body,
        mesh=mesh,
        in_specs=(
            P("lag", None, None, "space"),
            P("space"),
            P("space"),
            P(None, "space"),
            P("space"),
            P("space"),
            P(None, "space"),
            P(None, "space"),
            P(None, "space"),
        ),
        out_specs=P("lag", None, None, "space"),
        check_vma=False,
    )
```

```python
import jax
import jax.numpy as jnp
from jax import lax
from jax.experimental import pallas as pl
from jax.experimental.pallas import tpu as pltpu
from jax.sharding import PartitionSpec as P


K = 64
HALF = 64
ROWS = 80
UE = 64
UA = 64
UC = 64
INTERPRET = False
OBSERVE_BYTES = 12 << 20
SOLVE_BYTES = 24 << 20
F32 = jnp.float32
BF16 = jnp.bfloat16


def lanes_of(shape):
    return lax.broadcasted_iota(jnp.int32, shape, len(shape) - 1)


def dot(left, right):
    return jnp.dot(left, right, preferred_element_type=F32)


def stage_kernel(
    prior, coef, column, value, weight, lists,
    newest_out, coef_out, column_out, value_out, weight_out, lists_out,
    sems,
):
    lags = prior.shape[0]
    moves = (
        (prior.at[pl.ds(lags - 1, 1)], newest_out),
        (coef, coef_out),
        (column, column_out),
        (value, value_out),
        (weight, weight_out),
        (lists, lists_out),
    )
    copies = [pltpu.make_async_copy(a, b, sems.at[n]) for n, (a, b) in enumerate(moves)]
    for copy in copies:
        copy.start()
    for copy in copies:
        copy.wait()


def observe_kernel(
    flag, newest, coef, column, value, weight, lists, count, prior, index, local,
    own, first, second, prior_out, index_out, local_out, sems,
):
    moves = ((prior, prior_out), (index, index_out), (local, local_out))
    copies = [pltpu.make_async_copy(a, b, sems.at[n]) for n, (a, b) in enumerate(moves)]
    for copy in copies:
        copy.start()
    slots = column.shape[1]
    lags, spec = newest.shape[0], newest.shape[1]
    halo = lists.shape[1]
    hot = lax.broadcasted_iota(jnp.int32, (128, slots), 0) == column[...]
    hot = jnp.where(hot, 1.0, 0.0).astype(BF16)
    picked = dot(newest[lags - 1].reshape(spec * K, 128), hot)
    hx = coef[0:1, :] * picked[0:K]
    for s in range(1, spec):
        hx = hx + coef[s : s + 1, :] * picked[s * K : (s + 1) * K]
    mean = jnp.sum(hx, axis=0, keepdims=True) * (1.0 / K)
    valid = jnp.where(lanes_of((1, slots)) < count[:, 0:1], 1.0, 0.0)
    pert = (hx - mean) * valid
    info = jnp.concatenate(
        [weight[...] * valid, (value[...] - mean) * valid, jnp.zeros((ROWS - K - 2, slots), F32)],
        axis=0,
    )
    table = jnp.concatenate([pert, info], axis=0).astype(BF16)
    own[...] = table
    blocks = slots // 128
    stacked = jnp.concatenate([table[:, b * 128 : (b + 1) * 128] for b in range(blocks)], axis=0)
    odd = flag[0] == 1
    for out, mine, other in ((first, 0, 1), (second, 1, 0)):
        index = jnp.where(odd, lists[mine : mine + 1, :], lists[other : other + 1, :])
        low = index & 127
        high = index >> 7
        hot = lax.broadcasted_iota(jnp.int32, (128, halo), 0) == low
        found = dot(stacked, jnp.where(hot, 1.0, 0.0).astype(BF16))
        total = found[0:ROWS]
        for b in range(1, blocks):
            total = jnp.where(high == b, found[b * ROWS : (b + 1) * ROWS], total)
        out[...] = total.astype(BF16)
    for copy in copies:
        copy.wait()


def packed(square, lower):
    left = lanes_of((HALF, 128)) < HALF
    if lower:
        return jnp.where(left, square[0:HALF], pltpu.roll(square[HALF:], HALF, 1))
    return jnp.where(left, pltpu.roll(square[0:HALF], HALF, 1), square[HALF:])


def block_diagonal(pair, left):
    zero = jnp.zeros_like(pair)
    return jnp.concatenate([jnp.where(left, pair, zero), jnp.where(left, zero, pair)], axis=0)


def prepare_kernel(flag, index, local, prior, pd, means, weights, lows, codes):
    lags, spec = prior.shape[0], prior.shape[1]
    left = lanes_of((HALF, 128)) < HALF

    def beside(values):
        twice = jnp.concatenate([values, values], axis=0).T
        return jnp.where(left, twice[0:HALF], twice[HALF:])

    weights[...] = beside(local[...])
    places = beside(index[...].astype(F32)).astype(jnp.int32)
    block = places >> 8
    lows[...] = (places & 255).astype(F32)
    codes[...] = jnp.where(block >= 4, block ^ (2 * flag[0]), block)

    def rank(pair):
        lag, s = pair // spec, pair % spec
        values = prior[lag, s].astype(F32)
        mean = jnp.sum(values, axis=0, keepdims=True) * (1.0 / K)
        means[pair : pair + 1, :] = mean
        return (values - mean).astype(BF16).astype(F32)

    for pair in range(0, lags * spec, 2):
        square = jnp.concatenate([rank(pair), rank(pair + 1)], axis=0).T
        pd[pl.ds(pair, HALF, stride=8), :] = packed(square, True)
        pd[pl.ds(pair + 1, HALF, stride=8), :] = packed(square, False)


def apart(rows, pair):
    left = lanes_of((16, 128)) < HALF
    lhs = jnp.concatenate([rows, pltpu.roll(rows, HALF, 1)], axis=0)[:, 0:HALF].astype(BF16)
    product = dot(lhs, pair)
    return jnp.where(left, product[0:16], product[16:])


def gatherer(sources, codes_of, lows, codes):
    blocks = 8
    views = dict(zip(codes_of, (ref[:, b * 256 : (b + 1) * 256] for ref, b in sources)))
    zero = jnp.zeros((16, 256), F32)
    infos = [views[b][HALF : HALF + 16].astype(F32) if b in views else zero for b in range(blocks)]
    infos = [info[n : n + 1] for n in range(2) for info in infos]
    stacked = jnp.concatenate(
        [views[b][0:HALF] for b in codes_of] + [jnp.concatenate(infos, axis=0).astype(BF16)], axis=0
    )
    counts = lax.broadcasted_iota(jnp.int32, (256, 256), 0).astype(F32).astype(BF16)
    which = lax.broadcasted_iota(jnp.int32, (blocks, 256), 0)
    high, none = jnp.ones((256, 256), BF16), jnp.zeros((256, 256), BF16)
    tail = len(codes_of) * HALF

    def pick(q, total):
        low = jnp.concatenate([lows[pl.ds(q, 1), :], lows[pl.ds(q + 1, 1), :]], axis=1)
        code = jnp.concatenate([codes[pl.ds(q, 1), :], codes[pl.ds(q + 1, 1), :]], axis=1)
        found = dot(stacked, jnp.where(counts == low.astype(BF16), high, none))
        for n, b in enumerate(codes_of):
            part = found[n * HALF : (n + 1) * HALF]
            total = part if total is None else jnp.where(code == b, part, total)
        mine = which == code
        info = [
            jnp.sum(jnp.where(mine, found[at : at + blocks], 0.0), axis=0, keepdims=True)
            for at in (tail, tail + blocks)
        ]
        return [
            (total[:, at : at + 128], info[0][:, at : at + 128], info[1][:, at : at + 128])
            for at in (0, 128)
        ]

    return pick


def early_kernel(own, second, lows, codes, partial, info0_out, info1_out):
    pick = gatherer(
        [(own, b) for b in range(4)] + [(second, b) for b in range(2)],
        (0, 1, 2, 3, 6, 7), lows, codes,
    )

    @pl.loop(0, HALF // UE)
    def _(step):
        for u in range(0, UE, 2):
            q = step * UE + u
            for n, (total, info0, info1) in enumerate(pick(q, None)):
                partial[q + n] = total
                info0_out[pl.ds(q + n, 1), :] = info0
                info1_out[pl.ds(q + n, 1), :] = info1


def solve_kernel(
    first, partial, early0, early1, pd, means, weights, lows, codes, out,
    matrix, squares, factors, tails, mixed, shift,
):
    lags, spec = out.shape[0], out.shape[1]
    count = lags * spec
    left = lanes_of((HALF, 128)) < HALF
    row = lax.broadcasted_iota(jnp.int32, (HALF, 128), 0)
    eye = jnp.where(row == (lanes_of((HALF, 128)) & (HALF - 1)), K - 1.0, 0.0)
    leftb = lanes_of((HALF, 128)) < HALF
    ones = block_diagonal(jnp.ones((HALF, 128), F32), left).astype(BF16)
    pick = gatherer([(first, b) for b in range(2)], (4, 5), lows, codes)

    @pl.loop(0, HALF // UA)
    def _(step):
        qs = [step * UA + u for u in range(UA)]
        picked = []
        for q in qs[::2]:
            picked += pick(q, jnp.concatenate([partial[q], partial[q + 1]], axis=1))
        lefts, diagonals = [], []
        for q, (gathered, info0, info1) in zip(qs, picked):
            info0 = info0 + early0[pl.ds(q, 1), :]
            info1 = info1 + early1[pl.ds(q, 1), :]
            scaled = weights[pl.ds(q, 1), :] * info0
            weighted = (gathered * scaled).astype(BF16)
            pull = scaled * info1
            pull_high = pull.astype(BF16).astype(F32)
            extra = jnp.concatenate([pull_high, pull - pull_high, jnp.zeros((14, 128), F32)], axis=0)
            lefts.append(jnp.concatenate([weighted, extra.astype(BF16)], axis=0))
            diagonals.append(block_diagonal(gathered.astype(BF16), leftb))
        products = [
            lax.dot_general(l, d, (((1,), (1,)), ((), ())), preferred_element_type=F32)
            for l, d in zip(lefts, diagonals)
        ]
        for q, product in zip(qs, products):
            full = eye + product[0:HALF]
            matrix[q] = full
            squares[pl.ds(q, 1), :] = jnp.sum(full * full, axis=0, keepdims=True)
            drive = product[HALF : HALF + 1] + product[HALF + 1 : HALF + 2]
            drive_low = drive - drive.astype(BF16).astype(F32)
            tail = jnp.concatenate([drive, drive_low, jnp.zeros((6, 128), F32)], axis=0)
            tails[pl.ds(pl.multiple_of(q * 8, 8), 8), :] = tail

    def half_sums(values):
        high = values.astype(BF16)
        low = (values - high.astype(F32)).astype(BF16)
        return dot(high, ones) + dot(low, ones)

    scale = jnp.sqrt(half_sums(squares[...]))
    factors[...] = 1.0 / scale

    @pl.loop(0, HALF // UC)
    def _(step):
        qs = [step * UC + u for u in range(UC)]
        eights = [pl.ds(pl.multiple_of(q * 8, 8), 8) for q in qs]
        sides = [jnp.concatenate([pd[at, :], tails[at, :]], axis=0) for at in eights]
        halves = [(matrix[q] * factors[pl.ds(q, 1), :]).astype(BF16) for q in qs]
        low = [side.astype(BF16) for side in sides]
        once = [
            dot(jnp.concatenate([a, p], axis=0), block_diagonal(a, leftb))
            for a, p in zip(halves, low)
        ]
        seconds = [o[0:HALF].astype(BF16) for o in once]
        once = [o[HALF:] for o in once]
        twice = [apart(p, b) for p, b in zip(sides, seconds)]
        rest = [apart(t - 9.0 * o, b) for t, o, b in zip(twice, once, seconds)]
        for at, side, o, t, r in zip(eights, sides, once, twice, rest):
            product = 36.0 * side - 39.0 * o + 27.0 * t + r
            mix = product[0:8]
            pulled = product[8:9] + product[9:10]
            mixed[at, :] = mix
            shift[at, :] = mix * pulled

    shift[...] = half_sums(shift[...])
    one = factors[...]
    root = jnp.sqrt(one * (K - 1.0)) * (1.0 / 16.0)
    one = one * (1.0 / 256.0)

    def final(pair):
        at = pl.ds(pair, HALF, stride=8)
        return mixed[at, :] * root + shift[at, :] * one

    for pair in range(0, count, 2):
        square = jnp.concatenate([final(pair), final(pair + 1)], axis=0).T
        for which in range(2):
            lag, s = (pair + which) // spec, (pair + which) % spec
            value = packed(square, which == 0) + means[pair + which : pair + which + 1, :]
            out[lag, s] = value.astype(BF16)


def vmem():
    return pl.BlockSpec(memory_space=pltpu.VMEM)


def smem():
    return pl.BlockSpec(memory_space=pltpu.SMEM)


def anywhere():
    return pl.BlockSpec(memory_space=pltpu.HBM)


def stage(*args):
    prior, *rest = (pltpu.with_memory_space_constraint(x, pltpu.HBM) for x in args)
    shapes = [
        jax.ShapeDtypeStruct((1, *prior.shape[1:]), prior.dtype),
        *(jax.ShapeDtypeStruct(x.shape, x.dtype) for x in rest),
    ]
    return pl.pallas_call(
        stage_kernel,
        out_shape=shapes,
        in_specs=[anywhere()] * 6,
        out_specs=[vmem()] * 6,
        scratch_shapes=[pltpu.SemaphoreType.DMA((6,))],
        compiler_params=pltpu.CompilerParams(vmem_limit_bytes=OBSERVE_BYTES),
        interpret=INTERPRET,
        name="stage",
    )(prior, *rest)


def observe(flag, newest, coef, column, value, weight, lists, count, *later):
    slots, halo = column.shape[1], lists.shape[1]
    shapes = [(ROWS, slots), (ROWS, halo), (ROWS, halo)]
    later = [pltpu.with_memory_space_constraint(x, pltpu.HBM) for x in later]
    return pl.pallas_call(
        observe_kernel,
        out_shape=[jax.ShapeDtypeStruct(s, BF16) for s in shapes]
        + [jax.ShapeDtypeStruct(x.shape, x.dtype) for x in later],
        in_specs=[smem()] + [vmem()] * 7 + [anywhere()] * 3,
        out_specs=[vmem()] * 6,
        scratch_shapes=[pltpu.SemaphoreType.DMA((3,))],
        compiler_params=pltpu.CompilerParams(vmem_limit_bytes=OBSERVE_BYTES),
        interpret=INTERPRET,
        name="observe",
    )(flag, newest, coef, column, value, weight, lists, count, *later)


def prepare(flag, index, local, prior):
    ranks = prior.shape[0] * prior.shape[1]
    shapes = [
        jax.ShapeDtypeStruct((HALF * ranks, 128), F32),
        jax.ShapeDtypeStruct((ranks, 128), F32),
        jax.ShapeDtypeStruct((HALF, 128), F32),
        jax.ShapeDtypeStruct((HALF, 128), F32),
        jax.ShapeDtypeStruct((HALF, 128), jnp.int32),
    ]
    return pl.pallas_call(
        prepare_kernel,
        out_shape=shapes,
        in_specs=[smem()] + [vmem()] * 3,
        out_specs=[vmem()] * 5,
        compiler_params=pltpu.CompilerParams(vmem_limit_bytes=OBSERVE_BYTES),
        interpret=INTERPRET,
        name="prepare",
    )(flag, index, local, prior)


def early(own, second, lows, codes):
    shapes = [(HALF, HALF, 128), (HALF, 128), (HALF, 128)]
    return pl.pallas_call(
        early_kernel,
        out_shape=[jax.ShapeDtypeStruct(x, F32) for x in shapes],
        in_specs=[vmem()] * 4,
        out_specs=[vmem()] * 3,
        compiler_params=pltpu.CompilerParams(vmem_limit_bytes=SOLVE_BYTES),
        interpret=INTERPRET,
        name="early",
    )(own, second, lows, codes)


def solve(own, first, second, pd, means, weights, lows, codes, shape):
    partial = early(own, second, lows, codes)
    return pl.pallas_call(
        solve_kernel,
        out_shape=jax.ShapeDtypeStruct(shape, BF16),
        in_specs=[vmem()] * 9,
        out_specs=vmem(),
        scratch_shapes=[
            pltpu.VMEM((HALF, HALF, 128), F32),
            pltpu.VMEM((HALF, 128), F32),
            pltpu.VMEM((HALF, 128), F32),
            pltpu.VMEM((HALF * 8, 128), F32),
            pltpu.VMEM((HALF * 8, 128), F32),
            pltpu.VMEM((HALF * 8, 128), F32),
        ],
        compiler_params=pltpu.CompilerParams(vmem_limit_bytes=SOLVE_BYTES),
        interpret=INTERPRET,
        name="solve",
    )(first, *partial, pd, means, weights, lows, codes)


def swaps(length, start):
    pairs = []
    for low in range(start, length - 1, 2):
        pairs += [(low, low + 1), (low + 1, low)]
    return pairs


def body(
    prior,
    obs_value,
    obs_weight,
    obs_coef,
    obs_column,
    obs_count,
    halo_lists,
    neighbours,
    localization,
):
    tiles = lax.axis_size("space")
    flag = (lax.axis_index("space") % 2)[None].astype(jnp.int32)
    newest, *staged = stage(
        prior, obs_coef, obs_column[None], obs_value[None], obs_weight[None], halo_lists
    )
    newest = lax.all_gather(newest, "lag", axis=0, tiled=True)
    own, first, second, prior, index, local = observe(
        flag, newest, *staged, obs_count[None], prior, neighbours, localization
    )
    second = lax.ppermute(second, "space", swaps(tiles, 0))
    first = lax.ppermute(first, "space", swaps(tiles, 1))
    ready = prepare(flag, index, local, prior)
    return solve(own, first, second, *ready, prior.shape)


def solution(mesh):
    return jax.shard_map(
        body,
        mesh=mesh,
        in_specs=(
            P("lag", None, None, "space"),
            P("space"),
            P("space"),
            P(None, "space"),
            P("space"),
            P("space"),
            P(None, "space"),
            P(None, "space"),
            P(None, "space"),
        ),
        out_specs=P("lag", None, None, "space"),
        check_vma=False,
    )
```

```python
import jax
import jax.numpy as jnp
from jax import lax
from jax.experimental import pallas as pl
from jax.experimental.pallas import tpu as pltpu
from jax.sharding import PartitionSpec as P


K = 64
HALF = 64
ROWS = 80
UE = 64
UA = 64
UC = 64
INTERPRET = False
OBSERVE_BYTES = 12 << 20
SOLVE_BYTES = 24 << 20
F32 = jnp.float32
BF16 = jnp.bfloat16


def lanes_of(shape):
    return lax.broadcasted_iota(jnp.int32, shape, len(shape) - 1)


def dot(left, right):
    return jnp.dot(left, right, preferred_element_type=F32)


def stage_kernel(
    prior, coef, column, value, weight, lists,
    newest_out, coef_out, column_out, value_out, weight_out, lists_out,
    sems,
):
    lags = prior.shape[0]
    moves = (
        (prior.at[pl.ds(lags - 1, 1)], newest_out),
        (coef, coef_out),
        (column, column_out),
        (value, value_out),
        (weight, weight_out),
        (lists, lists_out),
    )
    copies = [pltpu.make_async_copy(a, b, sems.at[n]) for n, (a, b) in enumerate(moves)]
    for copy in copies:
        copy.start()
    for copy in copies:
        copy.wait()


def observe_kernel(
    flag, newest, coef, column, value, weight, lists, count, prior, index, local,
    own, first, second, prior_out, index_out, local_out, sems,
):
    moves = ((prior, prior_out), (index, index_out), (local, local_out))
    copies = [pltpu.make_async_copy(a, b, sems.at[n]) for n, (a, b) in enumerate(moves)]
    for copy in copies:
        copy.start()
    slots = column.shape[1]
    lags, spec = newest.shape[0], newest.shape[1]
    halo = lists.shape[1]
    hot = lax.broadcasted_iota(jnp.int32, (128, slots), 0) == column[...]
    hot = jnp.where(hot, 1.0, 0.0).astype(BF16)
    picked = dot(newest[lags - 1].reshape(spec * K, 128), hot)
    hx = coef[0:1, :] * picked[0:K]
    for s in range(1, spec):
        hx = hx + coef[s : s + 1, :] * picked[s * K : (s + 1) * K]
    mean = jnp.sum(hx, axis=0, keepdims=True) * (1.0 / K)
    valid = jnp.where(lanes_of((1, slots)) < count[:, 0:1], 1.0, 0.0)
    pert = (hx - mean) * valid
    info = jnp.concatenate(
        [weight[...] * valid, (value[...] - mean) * valid, jnp.zeros((ROWS - K - 2, slots), F32)],
        axis=0,
    )
    table = jnp.concatenate([pert, info], axis=0).astype(BF16)
    own[...] = table
    blocks = slots // 128
    stacked = jnp.concatenate([table[:, b * 128 : (b + 1) * 128] for b in range(blocks)], axis=0)
    odd = flag[0] == 1
    for out, mine, other in ((first, 0, 1), (second, 1, 0)):
        index = jnp.where(odd, lists[mine : mine + 1, :], lists[other : other + 1, :])
        low = index & 127
        high = index >> 7
        hot = lax.broadcasted_iota(jnp.int32, (128, halo), 0) == low
        found = dot(stacked, jnp.where(hot, 1.0, 0.0).astype(BF16))
        total = found[0:ROWS]
        for b in range(1, blocks):
            total = jnp.where(high == b, found[b * ROWS : (b + 1) * ROWS], total)
        out[...] = total.astype(BF16)
    for copy in copies:
        copy.wait()


def packed(square, lower):
    left = lanes_of((HALF, 128)) < HALF
    if lower:
        return jnp.where(left, square[0:HALF], pltpu.roll(square[HALF:], HALF, 1))
    return jnp.where(left, pltpu.roll(square[0:HALF], HALF, 1), square[HALF:])


def block_diagonal(pair, left):
    zero = jnp.zeros_like(pair)
    return jnp.concatenate([jnp.where(left, pair, zero), jnp.where(left, zero, pair)], axis=0)


def prepare_kernel(flag, index, local, prior, pd, means, weights, lows, codes):
    lags, spec = prior.shape[0], prior.shape[1]
    left = lanes_of((HALF, 128)) < HALF

    def beside(values):
        twice = jnp.concatenate([values, values], axis=0).T
        return jnp.where(left, twice[0:HALF], twice[HALF:])

    weights[...] = beside(local[...])
    places = beside(index[...].astype(F32)).astype(jnp.int32)
    block = places >> 8
    lows[...] = (places & 255).astype(F32)
    codes[...] = jnp.where(block >= 4, block ^ (2 * flag[0]), block)

    def rank(pair):
        lag, s = pair // spec, pair % spec
        values = prior[lag, s].astype(F32)
        mean = jnp.sum(values, axis=0, keepdims=True) * (1.0 / K)
        means[pair : pair + 1, :] = mean
        return (values - mean).astype(BF16).astype(F32)

    for pair in range(0, lags * spec, 2):
        square = jnp.concatenate([rank(pair), rank(pair + 1)], axis=0).T
        pd[pl.ds(pair, HALF, stride=8), :] = packed(square, True)
        pd[pl.ds(pair + 1, HALF, stride=8), :] = packed(square, False)


def apart(rows, pair):
    left = lanes_of((16, 128)) < HALF
    lhs = jnp.concatenate([rows, pltpu.roll(rows, HALF, 1)], axis=0)[:, 0:HALF].astype(BF16)
    product = dot(lhs, pair)
    return jnp.where(left, product[0:16], product[16:])


def gatherer(sources, codes_of, lows, codes, hots, fill):
    blocks = 8
    views = dict(zip(codes_of, (ref[:, b * 256 : (b + 1) * 256] for ref, b in sources)))
    zero = jnp.zeros((16, 256), F32)
    infos = [views[b][HALF : HALF + 16].astype(F32) if b in views else zero for b in range(blocks)]
    infos = [info[n : n + 1] for n in range(2) for info in infos]
    stacked = jnp.concatenate(
        [views[b][0:HALF] for b in codes_of] + [jnp.concatenate(infos, axis=0).astype(BF16)], axis=0
    )
    counts = lax.broadcasted_iota(jnp.int32, (256, 256), 0).astype(F32).astype(BF16)
    which = lax.broadcasted_iota(jnp.int32, (blocks, 256), 0)
    high, none = jnp.ones((256, 256), BF16), jnp.zeros((256, 256), BF16)
    tail = len(codes_of) * HALF

    def pick(q, total):
        low = jnp.concatenate([lows[pl.ds(q, 1), :], lows[pl.ds(q + 1, 1), :]], axis=1)
        code = jnp.concatenate([codes[pl.ds(q, 1), :], codes[pl.ds(q + 1, 1), :]], axis=1)
        half = pl.multiple_of(q // 2 * 256, 256) if not isinstance(q, int) else q // 2 * 256
        if fill:
            hot = jnp.where(counts == low.astype(BF16), high, none)
            hots[pl.ds(half, 256), :] = hot
        else:
            hot = hots[pl.ds(half, 256), :]
        found = dot(stacked, hot)
        for n, b in enumerate(codes_of):
            part = found[n * HALF : (n + 1) * HALF]
            total = part if total is None else jnp.where(code == b, part, total)
        mine = which == code
        info = [
            jnp.sum(jnp.where(mine, found[at : at + blocks], 0.0), axis=0, keepdims=True)
            for at in (tail, tail + blocks)
        ]
        return [
            (total[:, at : at + 128], info[0][:, at : at + 128], info[1][:, at : at + 128])
            for at in (0, 128)
        ]

    return pick


def early_kernel(own, second, lows, codes, partial, info0_out, info1_out, hots):
    pick = gatherer(
        [(own, b) for b in range(4)] + [(second, b) for b in range(2)],
        (0, 1, 2, 3, 6, 7), lows, codes, hots, True,
    )

    @pl.loop(0, HALF // UE)
    def _(step):
        for u in range(0, UE, 2):
            q = step * UE + u
            for n, (total, info0, info1) in enumerate(pick(q, None)):
                partial[q + n] = total
                info0_out[pl.ds(q + n, 1), :] = info0
                info1_out[pl.ds(q + n, 1), :] = info1


def solve_kernel(
    first, partial, early0, early1, hots, pd, means, weights, lows, codes, out,
    matrix, squares, factors, tails, mixed, shift,
):
    lags, spec = out.shape[0], out.shape[1]
    count = lags * spec
    left = lanes_of((HALF, 128)) < HALF
    row = lax.broadcasted_iota(jnp.int32, (HALF, 128), 0)
    eye = jnp.where(row == (lanes_of((HALF, 128)) & (HALF - 1)), K - 1.0, 0.0)
    leftb = lanes_of((HALF, 128)) < HALF
    ones = block_diagonal(jnp.ones((HALF, 128), F32), left).astype(BF16)
    own_half = (lanes_of((128, 128)) < HALF) == (
        lax.broadcasted_iota(jnp.int32, (128, 128), 0) < HALF
    )
    pick = gatherer([(first, b) for b in range(2)], (4, 5), lows, codes, hots, False)

    @pl.loop(0, HALF // UA)
    def _(step):
        qs = [step * UA + u for u in range(UA)]
        picked = []
        for q in qs[::2]:
            picked += pick(q, jnp.concatenate([partial[q], partial[q + 1]], axis=1))
        lefts, diagonals = [], []
        for q, (gathered, info0, info1) in zip(qs, picked):
            info0 = info0 + early0[pl.ds(q, 1), :]
            info1 = info1 + early1[pl.ds(q, 1), :]
            scaled = weights[pl.ds(q, 1), :] * info0
            weighted = (gathered * scaled).astype(BF16)
            pull = scaled * info1
            pull_high = pull.astype(BF16).astype(F32)
            extra = jnp.concatenate([pull_high, pull - pull_high, jnp.zeros((14, 128), F32)], axis=0)
            lefts.append(jnp.concatenate([weighted, extra.astype(BF16)], axis=0))
            member = gathered.astype(BF16)
            turned = jnp.concatenate([member, member], axis=0).T
            diagonals.append(jnp.where(own_half, turned, jnp.zeros_like(turned)))
        products = [
            dot(l, d) for l, d in zip(lefts, diagonals)
        ]
        for q, product in zip(qs, products):
            full = eye + product[0:HALF]
            matrix[q] = full
            squares[pl.ds(q, 1), :] = jnp.sum(full * full, axis=0, keepdims=True)
            drive = product[HALF : HALF + 1] + product[HALF + 1 : HALF + 2]
            drive_low = drive - drive.astype(BF16).astype(F32)
            tail = jnp.concatenate([drive, drive_low, jnp.zeros((6, 128), F32)], axis=0)
            tails[pl.ds(pl.multiple_of(q * 8, 8), 8), :] = tail

    def half_sums(values):
        high = values.astype(BF16)
        low = (values - high.astype(F32)).astype(BF16)
        return dot(high, ones) + dot(low, ones)

    scale = jnp.sqrt(half_sums(squares[...]))
    factors[...] = 1.0 / scale

    @pl.loop(0, HALF // UC)
    def _(step):
        qs = [step * UC + u for u in range(UC)]
        eights = [pl.ds(pl.multiple_of(q * 8, 8), 8) for q in qs]
        sides = [jnp.concatenate([pd[at, :], tails[at, :]], axis=0) for at in eights]
        halves = [(matrix[q] * factors[pl.ds(q, 1), :]).astype(BF16) for q in qs]
        low = [side.astype(BF16) for side in sides]
        once = [
            dot(jnp.concatenate([a, p], axis=0), block_diagonal(a, leftb))
            for a, p in zip(halves, low)
        ]
        seconds = [o[0:HALF].astype(BF16) for o in once]
        once = [o[HALF:] for o in once]
        twice = [apart(p, b) for p, b in zip(sides, seconds)]
        rest = [apart(t - 9.0 * o, b) for t, o, b in zip(twice, once, seconds)]
        for at, side, o, t, r in zip(eights, sides, once, twice, rest):
            product = 36.0 * side - 39.0 * o + 27.0 * t + r
            mix = product[0:8]
            pulled = product[8:9] + product[9:10]
            mixed[at, :] = mix
            shift[at, :] = mix * pulled

    shift[...] = half_sums(shift[...])
    one = factors[...]
    root = jnp.sqrt(one * (K - 1.0)) * (1.0 / 16.0)
    one = one * (1.0 / 256.0)

    def final(pair):
        at = pl.ds(pair, HALF, stride=8)
        return mixed[at, :] * root + shift[at, :] * one

    for pair in range(0, count, 2):
        square = jnp.concatenate([final(pair), final(pair + 1)], axis=0).T
        for which in range(2):
            lag, s = (pair + which) // spec, (pair + which) % spec
            value = packed(square, which == 0) + means[pair + which : pair + which + 1, :]
            out[lag, s] = value.astype(BF16)


def vmem():
    return pl.BlockSpec(memory_space=pltpu.VMEM)


def smem():
    return pl.BlockSpec(memory_space=pltpu.SMEM)


def anywhere():
    return pl.BlockSpec(memory_space=pltpu.HBM)


def stage(*args):
    prior, *rest = (pltpu.with_memory_space_constraint(x, pltpu.HBM) for x in args)
    shapes = [
        jax.ShapeDtypeStruct((1, *prior.shape[1:]), prior.dtype),
        *(jax.ShapeDtypeStruct(x.shape, x.dtype) for x in rest),
    ]
    return pl.pallas_call(
        stage_kernel,
        out_shape=shapes,
        in_specs=[anywhere()] * 6,
        out_specs=[vmem()] * 6,
        scratch_shapes=[pltpu.SemaphoreType.DMA((6,))],
        compiler_params=pltpu.CompilerParams(vmem_limit_bytes=OBSERVE_BYTES),
        interpret=INTERPRET,
        name="stage",
    )(prior, *rest)


def observe(flag, newest, coef, column, value, weight, lists, count, *later):
    slots, halo = column.shape[1], lists.shape[1]
    shapes = [(ROWS, slots), (ROWS, halo), (ROWS, halo)]
    later = [pltpu.with_memory_space_constraint(x, pltpu.HBM) for x in later]
    return pl.pallas_call(
        observe_kernel,
        out_shape=[jax.ShapeDtypeStruct(s, BF16) for s in shapes]
        + [jax.ShapeDtypeStruct(x.shape, x.dtype) for x in later],
        in_specs=[smem()] + [vmem()] * 7 + [anywhere()] * 3,
        out_specs=[vmem()] * 6,
        scratch_shapes=[pltpu.SemaphoreType.DMA((3,))],
        compiler_params=pltpu.CompilerParams(vmem_limit_bytes=OBSERVE_BYTES),
        interpret=INTERPRET,
        name="observe",
    )(flag, newest, coef, column, value, weight, lists, count, *later)


def prepare(flag, index, local, prior):
    ranks = prior.shape[0] * prior.shape[1]
    shapes = [
        jax.ShapeDtypeStruct((HALF * ranks, 128), F32),
        jax.ShapeDtypeStruct((ranks, 128), F32),
        jax.ShapeDtypeStruct((HALF, 128), F32),
        jax.ShapeDtypeStruct((HALF, 128), F32),
        jax.ShapeDtypeStruct((HALF, 128), jnp.int32),
    ]
    return pl.pallas_call(
        prepare_kernel,
        out_shape=shapes,
        in_specs=[smem()] + [vmem()] * 3,
        out_specs=[vmem()] * 5,
        compiler_params=pltpu.CompilerParams(vmem_limit_bytes=OBSERVE_BYTES),
        interpret=INTERPRET,
        name="prepare",
    )(flag, index, local, prior)


def early(own, second, lows, codes):
    shapes = [(HALF, HALF, 128), (HALF, 128), (HALF, 128)]
    return pl.pallas_call(
        early_kernel,
        out_shape=[jax.ShapeDtypeStruct(x, F32) for x in shapes]
        + [jax.ShapeDtypeStruct((HALF // 2 * 256, 256), BF16)],
        in_specs=[vmem()] * 4,
        out_specs=[vmem()] * 4,
        compiler_params=pltpu.CompilerParams(vmem_limit_bytes=SOLVE_BYTES),
        interpret=INTERPRET,
        name="early",
    )(own, second, lows, codes)


def solve(own, first, second, pd, means, weights, lows, codes, shape):
    partial = early(own, second, lows, codes)
    return pl.pallas_call(
        solve_kernel,
        out_shape=jax.ShapeDtypeStruct(shape, BF16),
        in_specs=[vmem()] * 10,
        out_specs=vmem(),
        scratch_shapes=[
            pltpu.VMEM((HALF, HALF, 128), F32),
            pltpu.VMEM((HALF, 128), F32),
            pltpu.VMEM((HALF, 128), F32),
            pltpu.VMEM((HALF * 8, 128), F32),
            pltpu.VMEM((HALF * 8, 128), F32),
            pltpu.VMEM((HALF * 8, 128), F32),
        ],
        compiler_params=pltpu.CompilerParams(vmem_limit_bytes=SOLVE_BYTES),
        interpret=INTERPRET,
        name="solve",
    )(first, *partial, pd, means, weights, lows, codes)


def swaps(length, start):
    pairs = []
    for low in range(start, length - 1, 2):
        pairs += [(low, low + 1), (low + 1, low)]
    return pairs


def body(
    prior,
    obs_value,
    obs_weight,
    obs_coef,
    obs_column,
    obs_count,
    halo_lists,
    neighbours,
    localization,
):
    tiles = lax.axis_size("space")
    flag = (lax.axis_index("space") % 2)[None].astype(jnp.int32)
    newest, *staged = stage(
        prior, obs_coef, obs_column[None], obs_value[None], obs_weight[None], halo_lists
    )
    newest = lax.all_gather(newest, "lag", axis=0, tiled=True)
    own, first, second, prior, index, local = observe(
        flag, newest, *staged, obs_count[None], prior, neighbours, localization
    )
    second = lax.ppermute(second, "space", swaps(tiles, 0))
    first = lax.ppermute(first, "space", swaps(tiles, 1))
    ready = prepare(flag, index, local, prior)
    return solve(own, first, second, *ready, prior.shape)


def solution(mesh):
    return jax.shard_map(
        body,
        mesh=mesh,
        in_specs=(
            P("lag", None, None, "space"),
            P("space"),
            P("space"),
            P(None, "space"),
            P("space"),
            P("space"),
            P(None, "space"),
            P(None, "space"),
            P(None, "space"),
        ),
        out_specs=P("lag", None, None, "space"),
        check_vma=False,
    )
```

```python
import jax
import jax.numpy as jnp
from jax import lax
from jax.experimental import pallas as pl
from jax.experimental.pallas import tpu as pltpu
from jax.sharding import PartitionSpec as P


K = 64
HALF = 64
ROWS = 80
UE = 64
UA = 64
UC = 64
INTERPRET = False
OBSERVE_BYTES = 12 << 20
SOLVE_BYTES = 24 << 20
F32 = jnp.float32
BF16 = jnp.bfloat16


def lanes_of(shape):
    return lax.broadcasted_iota(jnp.int32, shape, len(shape) - 1)


def dot(left, right):
    return jnp.dot(left, right, preferred_element_type=F32)


def stage_kernel(
    prior, coef, column, value, weight, lists, index, local,
    newest_out, older_out, coef_out, column_out, value_out, weight_out, lists_out,
    index_out, local_out, sems,
):
    lags = prior.shape[0]
    moves = (
        (prior.at[pl.ds(lags - 1, 1)], newest_out),
        (coef, coef_out),
        (column, column_out),
        (value, value_out),
        (weight, weight_out),
        (lists, lists_out),
        (prior.at[pl.ds(0, lags - 1)], older_out),
        (index, index_out),
        (local, local_out),
    )
    copies = [pltpu.make_async_copy(a, b, sems.at[n]) for n, (a, b) in enumerate(moves)]
    for copy in copies:
        copy.start()
    for copy in copies:
        copy.wait()


def observe_kernel(
    flag, newest, coef, column, value, weight, lists, count, own, first, second
):
    slots = column.shape[1]
    lags, spec = newest.shape[0], newest.shape[1]
    halo = lists.shape[1]
    hot = lax.broadcasted_iota(jnp.int32, (128, slots), 0) == column[...]
    hot = jnp.where(hot, 1.0, 0.0).astype(BF16)
    picked = dot(newest[lags - 1].reshape(spec * K, 128), hot)
    hx = coef[0:1, :] * picked[0:K]
    for s in range(1, spec):
        hx = hx + coef[s : s + 1, :] * picked[s * K : (s + 1) * K]
    mean = jnp.sum(hx, axis=0, keepdims=True) * (1.0 / K)
    valid = jnp.where(lanes_of((1, slots)) < count[:, 0:1], 1.0, 0.0)
    pert = (hx - mean) * valid
    info = jnp.concatenate(
        [weight[...] * valid, (value[...] - mean) * valid, jnp.zeros((ROWS - K - 2, slots), F32)],
        axis=0,
    )
    table = jnp.concatenate([pert, info], axis=0).astype(BF16)
    own[...] = table
    blocks = slots // 128
    stacked = jnp.concatenate([table[:, b * 128 : (b + 1) * 128] for b in range(blocks)], axis=0)
    odd = flag[0] == 1
    for out, mine, other in ((first, 0, 1), (second, 1, 0)):
        index = jnp.where(odd, lists[mine : mine + 1, :], lists[other : other + 1, :])
        low = index & 127
        high = index >> 7
        hot = lax.broadcasted_iota(jnp.int32, (128, halo), 0) == low
        found = dot(stacked, jnp.where(hot, 1.0, 0.0).astype(BF16))
        total = found[0:ROWS]
        for b in range(1, blocks):
            total = jnp.where(high == b, found[b * ROWS : (b + 1) * ROWS], total)
        out[...] = total.astype(BF16)


def packed(square, lower):
    left = lanes_of((HALF, 128)) < HALF
    if lower:
        return jnp.where(left, square[0:HALF], pltpu.roll(square[HALF:], HALF, 1))
    return jnp.where(left, pltpu.roll(square[0:HALF], HALF, 1), square[HALF:])


def block_diagonal(pair, left):
    zero = jnp.zeros_like(pair)
    return jnp.concatenate([jnp.where(left, pair, zero), jnp.where(left, zero, pair)], axis=0)


def prepare_kernel(flag, index, local, older, latest, pd, means, weights, lows, codes):
    lags, spec = older.shape[0] + 1, older.shape[1]
    left = lanes_of((HALF, 128)) < HALF

    def beside(values):
        twice = jnp.concatenate([values, values], axis=0).T
        return jnp.where(left, twice[0:HALF], twice[HALF:])

    weights[...] = beside(local[...])
    places = beside(index[...].astype(F32)).astype(jnp.int32)
    block = places >> 8
    lows[...] = (places & 255).astype(F32)
    codes[...] = jnp.where(block >= 4, block ^ (2 * flag[0]), block)

    def rank(pair):
        lag, s = pair // spec, pair % spec
        values = (latest[0, s] if lag == lags - 1 else older[lag, s]).astype(F32)
        mean = jnp.sum(values, axis=0, keepdims=True) * (1.0 / K)
        means[pair : pair + 1, :] = mean
        return (values - mean).astype(BF16).astype(F32)

    for pair in range(0, lags * spec, 2):
        square = jnp.concatenate([rank(pair), rank(pair + 1)], axis=0).T
        pd[pl.ds(pair, HALF, stride=8), :] = packed(square, True)
        pd[pl.ds(pair + 1, HALF, stride=8), :] = packed(square, False)


def apart(rows, pair):
    left = lanes_of((16, 128)) < HALF
    lhs = jnp.concatenate([rows, pltpu.roll(rows, HALF, 1)], axis=0)[:, 0:HALF].astype(BF16)
    product = dot(lhs, pair)
    return jnp.where(left, product[0:16], product[16:])


def gatherer(sources, codes_of, lows, codes, hots, fill):
    blocks = 8
    views = dict(zip(codes_of, (ref[:, b * 256 : (b + 1) * 256] for ref, b in sources)))
    zero = jnp.zeros((16, 256), F32)
    infos = [views[b][HALF : HALF + 16].astype(F32) if b in views else zero for b in range(blocks)]
    infos = [info[n : n + 1] for n in range(2) for info in infos]
    stacked = jnp.concatenate(
        [views[b][0:HALF] for b in codes_of] + [jnp.concatenate(infos, axis=0).astype(BF16)], axis=0
    )
    counts = lax.broadcasted_iota(jnp.int32, (256, 256), 0).astype(F32).astype(BF16)
    which = lax.broadcasted_iota(jnp.int32, (blocks, 256), 0)
    high, none = jnp.ones((256, 256), BF16), jnp.zeros((256, 256), BF16)
    tail = len(codes_of) * HALF

    def pick(q, total):
        low = jnp.concatenate([lows[pl.ds(q, 1), :], lows[pl.ds(q + 1, 1), :]], axis=1)
        code = jnp.concatenate([codes[pl.ds(q, 1), :], codes[pl.ds(q + 1, 1), :]], axis=1)
        half = pl.multiple_of(q // 2 * 256, 256) if not isinstance(q, int) else q // 2 * 256
        if fill:
            hot = jnp.where(counts == low.astype(BF16), high, none)
            hots[pl.ds(half, 256), :] = hot
        else:
            hot = hots[pl.ds(half, 256), :]
        found = dot(stacked, hot)
        for n, b in enumerate(codes_of):
            part = found[n * HALF : (n + 1) * HALF]
            total = part if total is None else jnp.where(code == b, part, total)
        mine = which == code
        info = [
            jnp.sum(jnp.where(mine, found[at : at + blocks], 0.0), axis=0, keepdims=True)
            for at in (tail, tail + blocks)
        ]
        return [
            (total[:, at : at + 128], info[0][:, at : at + 128], info[1][:, at : at + 128])
            for at in (0, 128)
        ]

    return pick


def early_kernel(own, second, lows, codes, partial, info0_out, info1_out, hots):
    pick = gatherer(
        [(own, b) for b in range(4)] + [(second, b) for b in range(2)],
        (0, 1, 2, 3, 6, 7), lows, codes, hots, True,
    )

    @pl.loop(0, HALF // UE)
    def _(step):
        for u in range(0, UE, 2):
            q = step * UE + u
            for n, (total, info0, info1) in enumerate(pick(q, None)):
                partial[q + n] = total
                info0_out[pl.ds(q + n, 1), :] = info0
                info1_out[pl.ds(q + n, 1), :] = info1


def solve_kernel(
    first, partial, early0, early1, hots, pd, means, weights, lows, codes, out,
    matrix, squares, factors, tails, mixed, shift,
):
    lags, spec = out.shape[0], out.shape[1]
    count = lags * spec
    left = lanes_of((HALF, 128)) < HALF
    row = lax.broadcasted_iota(jnp.int32, (HALF, 128), 0)
    eye = jnp.where(row == (lanes_of((HALF, 128)) & (HALF - 1)), K - 1.0, 0.0)
    leftb = lanes_of((HALF, 128)) < HALF
    ones = block_diagonal(jnp.ones((HALF, 128), F32), left).astype(BF16)
    own_half = (lanes_of((128, 128)) < HALF) == (
        lax.broadcasted_iota(jnp.int32, (128, 128), 0) < HALF
    )
    pick = gatherer([(first, b) for b in range(2)], (4, 5), lows, codes, hots, False)

    @pl.loop(0, HALF // UA)
    def _(step):
        qs = [step * UA + u for u in range(UA)]
        picked = []
        for q in qs[::2]:
            picked += pick(q, jnp.concatenate([partial[q], partial[q + 1]], axis=1))
        lefts, diagonals = [], []
        for q, (gathered, info0, info1) in zip(qs, picked):
            info0 = info0 + early0[pl.ds(q, 1), :]
            info1 = info1 + early1[pl.ds(q, 1), :]
            scaled = weights[pl.ds(q, 1), :] * info0
            weighted = (gathered * scaled).astype(BF16)
            pull = scaled * info1
            pull_high = pull.astype(BF16).astype(F32)
            extra = jnp.concatenate([pull_high, pull - pull_high, jnp.zeros((14, 128), F32)], axis=0)
            lefts.append(jnp.concatenate([weighted, extra.astype(BF16)], axis=0))
            member = gathered.astype(BF16)
            turned = jnp.concatenate([member, member], axis=0).T
            diagonals.append(jnp.where(own_half, turned, jnp.zeros_like(turned)))
        products = [
            dot(l, d) for l, d in zip(lefts, diagonals)
        ]
        for q, product in zip(qs, products):
            full = eye + product[0:HALF]
            matrix[q] = full
            squares[pl.ds(q, 1), :] = jnp.sum(full * full, axis=0, keepdims=True)
            drive = product[HALF : HALF + 1] + product[HALF + 1 : HALF + 2]
            drive_low = drive - drive.astype(BF16).astype(F32)
            tail = jnp.concatenate([drive, drive_low, jnp.zeros((6, 128), F32)], axis=0)
            tails[pl.ds(pl.multiple_of(q * 8, 8), 8), :] = tail

    def half_sums(values):
        high = values.astype(BF16)
        low = (values - high.astype(F32)).astype(BF16)
        return dot(jnp.concatenate([high, low], axis=1), jnp.concatenate([ones, ones], axis=0))

    scale = jnp.sqrt(half_sums(squares[...]))
    factors[...] = 1.0 / scale

    @pl.loop(0, HALF // UC)
    def _(step):
        qs = [step * UC + u for u in range(UC)]
        eights = [pl.ds(pl.multiple_of(q * 8, 8), 8) for q in qs]
        sides = [jnp.concatenate([pd[at, :], tails[at, :]], axis=0) for at in eights]
        halves = [(matrix[q] * factors[pl.ds(q, 1), :]).astype(BF16) for q in qs]
        low = [side.astype(BF16) for side in sides]
        once = [
            dot(jnp.concatenate([a, p], axis=0), block_diagonal(a, leftb))
            for a, p in zip(halves, low)
        ]
        seconds = [o[0:HALF].astype(BF16) for o in once]
        once = [o[HALF:] for o in once]
        twice = [apart(p, b) for p, b in zip(sides, seconds)]
        rest = [apart(t - 9.0 * o, b) for t, o, b in zip(twice, once, seconds)]
        for at, side, o, t, r in zip(eights, sides, once, twice, rest):
            product = 36.0 * side - 39.0 * o + 27.0 * t + r
            mix = product[0:8]
            pulled = product[8:9] + product[9:10]
            mixed[at, :] = mix
            shift[at, :] = mix * pulled

    shift[...] = half_sums(shift[...])
    one = factors[...]
    root = jnp.sqrt(one * (K - 1.0)) * (1.0 / 16.0)
    one = one * (1.0 / 256.0)

    def final(pair):
        at = pl.ds(pair, HALF, stride=8)
        return mixed[at, :] * root + shift[at, :] * one

    for pair in range(0, count, 2):
        square = jnp.concatenate([final(pair), final(pair + 1)], axis=0).T
        for which in range(2):
            lag, s = (pair + which) // spec, (pair + which) % spec
            value = packed(square, which == 0) + means[pair + which : pair + which + 1, :]
            out[lag, s] = value.astype(BF16)


def vmem():
    return pl.BlockSpec(memory_space=pltpu.VMEM)


def smem():
    return pl.BlockSpec(memory_space=pltpu.SMEM)


def anywhere():
    return pl.BlockSpec(memory_space=pltpu.HBM)


def stage(*args):
    prior, *rest = (pltpu.with_memory_space_constraint(x, pltpu.HBM) for x in args)
    shapes = [
        jax.ShapeDtypeStruct((1, *prior.shape[1:]), prior.dtype),
        jax.ShapeDtypeStruct((prior.shape[0] - 1, *prior.shape[1:]), prior.dtype),
        *(jax.ShapeDtypeStruct(x.shape, x.dtype) for x in rest),
    ]
    return pl.pallas_call(
        stage_kernel,
        out_shape=shapes,
        in_specs=[anywhere()] * 8,
        out_specs=[vmem()] * 9,
        scratch_shapes=[pltpu.SemaphoreType.DMA((9,))],
        compiler_params=pltpu.CompilerParams(vmem_limit_bytes=OBSERVE_BYTES),
        interpret=INTERPRET,
        name="stage",
    )(prior, *rest)


def observe(flag, newest, coef, column, value, weight, lists, count):
    slots, halo = column.shape[1], lists.shape[1]
    shapes = [(ROWS, slots), (ROWS, halo), (ROWS, halo)]
    return pl.pallas_call(
        observe_kernel,
        out_shape=[jax.ShapeDtypeStruct(s, BF16) for s in shapes],
        in_specs=[smem()] + [vmem()] * 7,
        out_specs=[vmem()] * 3,
        compiler_params=pltpu.CompilerParams(vmem_limit_bytes=OBSERVE_BYTES),
        interpret=INTERPRET,
        name="observe",
    )(flag, newest, coef, column, value, weight, lists, count)


def prepare(flag, index, local, older, latest):
    ranks = (older.shape[0] + 1) * older.shape[1]
    shapes = [
        jax.ShapeDtypeStruct((HALF * ranks, 128), F32),
        jax.ShapeDtypeStruct((ranks, 128), F32),
        jax.ShapeDtypeStruct((HALF, 128), F32),
        jax.ShapeDtypeStruct((HALF, 128), F32),
        jax.ShapeDtypeStruct((HALF, 128), jnp.int32),
    ]
    return pl.pallas_call(
        prepare_kernel,
        out_shape=shapes,
        in_specs=[smem()] + [vmem()] * 4,
        out_specs=[vmem()] * 5,
        compiler_params=pltpu.CompilerParams(vmem_limit_bytes=OBSERVE_BYTES),
        interpret=INTERPRET,
        name="prepare",
    )(flag, index, local, older, latest)


def early(own, second, lows, codes):
    shapes = [(HALF, HALF, 128), (HALF, 128), (HALF, 128)]
    return pl.pallas_call(
        early_kernel,
        out_shape=[jax.ShapeDtypeStruct(x, F32) for x in shapes]
        + [jax.ShapeDtypeStruct((HALF // 2 * 256, 256), BF16)],
        in_specs=[vmem()] * 4,
        out_specs=[vmem()] * 4,
        compiler_params=pltpu.CompilerParams(vmem_limit_bytes=SOLVE_BYTES),
        interpret=INTERPRET,
        name="early",
    )(own, second, lows, codes)


def solve(own, first, second, pd, means, weights, lows, codes, shape):
    partial = early(own, second, lows, codes)
    return pl.pallas_call(
        solve_kernel,
        out_shape=jax.ShapeDtypeStruct(shape, BF16),
        in_specs=[vmem()] * 10,
        out_specs=vmem(),
        scratch_shapes=[
            pltpu.VMEM((HALF, HALF, 128), F32),
            pltpu.VMEM((HALF, 128), F32),
            pltpu.VMEM((HALF, 128), F32),
            pltpu.VMEM((HALF * 8, 128), F32),
            pltpu.VMEM((HALF * 8, 128), F32),
            pltpu.VMEM((HALF * 8, 128), F32),
        ],
        compiler_params=pltpu.CompilerParams(vmem_limit_bytes=SOLVE_BYTES),
        interpret=INTERPRET,
        name="solve",
    )(first, *partial, pd, means, weights, lows, codes)


def swaps(length, start):
    pairs = []
    for low in range(start, length - 1, 2):
        pairs += [(low, low + 1), (low + 1, low)]
    return pairs


def body(
    prior,
    obs_value,
    obs_weight,
    obs_coef,
    obs_column,
    obs_count,
    halo_lists,
    neighbours,
    localization,
):
    tiles = lax.axis_size("space")
    flag = (lax.axis_index("space") % 2)[None].astype(jnp.int32)
    latest, older, *staged, index, local = stage(
        prior, obs_coef, obs_column[None], obs_value[None], obs_weight[None], halo_lists,
        neighbours, localization,
    )
    newest = lax.all_gather(latest, "lag", axis=0, tiled=True)
    own, first, second = observe(flag, newest, *staged, obs_count[None])
    second = lax.ppermute(second, "space", swaps(tiles, 0))
    first = lax.ppermute(first, "space", swaps(tiles, 1))
    ready = prepare(flag, index, local, older, latest)
    return solve(own, first, second, *ready, prior.shape)


def solution(mesh):
    return jax.shard_map(
        body,
        mesh=mesh,
        in_specs=(
            P("lag", None, None, "space"),
            P("space"),
            P("space"),
            P(None, "space"),
            P("space"),
            P("space"),
            P(None, "space"),
            P(None, "space"),
            P(None, "space"),
        ),
        out_specs=P("lag", None, None, "space"),
        check_vma=False,
    )
```
